32 devices in a mesh: trow: 4 (over y, x), tcol: 4 (over z), tm: 2 (over core).
Axes of the slice: x: 2, y: 2, z: 4, core: 2. Of those that a mesh axis runs over, the one named last changes fastest.
Arguments:
- start_field: float32 [2, 2, 8, 4096], P('tm', None, None, 'tcol'), may hold values from -6 to 6
- u_tiles: bfloat16 [2, 2, 4096, 2048], P('tm', None, 'trow', 'tcol'), may hold values from -0.25 to 0.25
- v_tiles: bfloat16 [2, 2, 2048, 4096], P('tm', None, 'trow', 'tcol'), may hold values from -0.0546875 to 0.0546875
- rank_blocks: int32 [2, 4, 4], P('tm', 'trow', 'tcol'), may hold values from 1 to 2
- onset_receiver: int32 [8, 4096], P(None, 'trow'), may hold values from 128 to 1023
- onset_source: int32 [8, 4096], P(None, 'tcol'), may hold values from 128 to 1023
- omega: float32 [2], replicated, may hold values from 0.1 to 0.9
Outputs:
- plus_field: float32 [2, 2, 8, 4096], P('tm', None, None, 'tcol')
- minus_field: bfloat16 [2, 2, 8, 4096], P('tm', None, None, 'trow')
The draws below stay inside these ranges and needn't reach their ends.
Inputs may be any that keep to these rules, and one draw needn't show every extreme that they name: `rank_blocks`: tiles use whole rank blocks; a tile with the most uses all 512 columns.
All inputs are finite; a program needn't handle non-finite values.
Results may differ from the reference program's by a relative error of at most 0.01.
Values may be sent and summed in bfloat16 or wider, within the bound.
A program may use at most 64 MiB of HBM per device.

```python
import jax
import jax.numpy as jnp
from jax import lax

TILE = 1024
RBLK = 256
RBMAX = 2
RMAX = 512
NV = 8
NT = 1024
ITERS = 1
NFQ = 2
NR = 4096
NS = 4096
N_TROW = 4
N_TCOL = 4


def with_ends(result, own_key, least, high):
    dims = result.shape
    spot = [jax.random.randint(jax.random.fold_in(own_key, axis), (), 0, dims[axis]) for axis in range(len(dims))]
    result = result.at[tuple(spot)].set(least)
    longest = dims.index(max(dims))
    spot[longest] = (spot[longest] + 1) % dims[longest]
    return result.at[tuple(spot)].set(high)


def block_scale(rng, shape, cuts, low, top_value):
    def one(axis_at, parts):
        heights = jax.random.uniform(jax.random.fold_in(jax.random.fold_in(rng, 6), axis_at), (parts,), jnp.float32, low / len(cuts), top_value / len(cuts))
        return jnp.repeat(jnp.exp(heights), shape[axis_at] // parts).reshape((-1,) + (1,) * (len(shape) - axis_at - 1))

    factor_of = one(*cuts[0])
    for cut in cuts[1:]:
        factor_of = factor_of * one(*cut)
    return factor_of


def bell_draw(own_key, shape, deviation, reach, split=(), kind=jnp.bfloat16):
    drawn = deviation * jax.random.normal(own_key, shape, jnp.float32)
    if split:
        drawn = drawn * block_scale(own_key, shape, split, -0.22, 0.18)
    return jnp.clip(drawn, -reach, reach).astype(kind)


def setup_inputs(seed: int = 0) -> dict:
    streams_of = jax.random.split(jax.random.key(seed), 8)
    start_field = bell_draw(streams_of[0], (NFQ, 2, NV, NS), 1.0, 6.0, ((0, 2), (3, 4)), jnp.float32)
    u_tiles = bell_draw(streams_of[1], (NFQ, 2, NR, N_TCOL * RMAX), RMAX ** -0.5, 0.25, ((0, 2), (2, 4), (3, 4)))
    v_tiles = bell_draw(streams_of[2], (NFQ, 2, N_TROW * RMAX, NS), ((4 * (NR + NS)) // 3) ** -0.5, 0.0546875, ((0, 2), (2, 4), (3, 4)))
    rank_blocks = with_ends(jax.random.randint(streams_of[3], (NFQ, N_TROW, N_TCOL), 1, RBMAX + 1), jax.random.fold_in(streams_of[3], 1), 1, RBMAX).astype(jnp.int32)
    onset_receiver = with_ends(jax.random.randint(streams_of[4], (NV, NR), NT // 8, NT), jax.random.fold_in(streams_of[4], 1), NT // 8, NT - 1).astype(jnp.int32)
    onset_source = with_ends(jax.random.randint(streams_of[5], (NV, NS), NT // 8, NT), jax.random.fold_in(streams_of[5], 1), NT // 8, NT - 1).astype(jnp.int32)
    omega = jnp.clip(jax.random.uniform(streams_of[6], (NFQ,), jnp.float32, 0.1, 0.9), 0.1, 0.9)
    return dict(start_field=start_field, u_tiles=u_tiles, v_tiles=v_tiles, rank_blocks=rank_blocks, onset_receiver=onset_receiver, onset_source=onset_source, omega=omega)


HIGHEST = lax.Precision.HIGHEST


def rounded(array_value):
    return lax.optimization_barrier(array_value.astype(jnp.bfloat16)).astype(jnp.float32)


def product(form, left_side, right_side):
    return jnp.einsum(form, left_side, right_side, precision=HIGHEST)


def window_field(field, onset, omega):
    time_grid = jnp.arange(NT, dtype=jnp.float32)
    time_index = jnp.arange(NT, dtype=jnp.int32)
    phase_grid = omega[:, None] * time_grid[None, :]
    cosine = jnp.cos(phase_grid)
    sine_table = jnp.sin(phase_grid)
    synth_basis = jnp.stack([cosine, -sine_table], axis=1).reshape(2 * NFQ, NT)
    by_point = jnp.transpose(field, (2, 0, 1, 3))

    def per_point(point_pair):
        field_part, limits = point_pair
        coefficients = field_part.reshape(2 * NFQ, field_part.shape[-1])
        traces = jnp.dot(coefficients.T, synth_basis, precision=HIGHEST, preferred_element_type=jnp.float32)
        keep_mask = time_index[None, :] < limits[:, None]
        traces = jnp.where(keep_mask, traces, jnp.zeros_like(traces))
        real_part = jnp.dot(traces, cosine.T, precision=HIGHEST, preferred_element_type=jnp.float32) * (2.0 / NT)
        imag_part = -jnp.dot(traces, sine_table.T, precision=HIGHEST, preferred_element_type=jnp.float32) * (2.0 / NT)
        return jnp.stack([real_part.T, imag_part.T], axis=1)

    windowed = lax.map(per_point, (by_point, onset))
    return jnp.transpose(windowed, (1, 2, 0, 3))


def row_factors(u_tiles, v_tiles, rank_blocks, row_index):
    u_rows = lax.dynamic_slice_in_dim(u_tiles, row_index * TILE, TILE, axis=2).astype(jnp.float32)
    u_rows = u_rows.reshape(NFQ, 2, TILE, N_TCOL, RMAX)
    v_rows = lax.dynamic_slice_in_dim(v_tiles, row_index * RMAX, RMAX, axis=2).astype(jnp.float32)
    v_rows = v_rows.reshape(NFQ, 2, RMAX, N_TCOL, TILE)
    blocks = lax.dynamic_index_in_dim(rank_blocks, row_index, axis=1, keepdims=False)
    rank_index = jnp.arange(RMAX, dtype=jnp.int32)
    live_mask = (rank_index[None, None, :] < blocks[:, :, None] * RBLK).astype(jnp.float32)
    return u_rows, v_rows, live_mask[:, None]


def forward_apply(field, u_tiles, v_tiles, rank_blocks):
    field_in = rounded(field).reshape(NFQ, 2, NV, N_TCOL, TILE)

    def one_row(row_index):
        u_rows, v_rows, live_mask = row_factors(u_tiles, v_tiles, rank_blocks, row_index)
        form = 'kvbj,krbj->kvbr'
        t_real = product(form, field_in[:, 0], v_rows[:, 0]) - product(form, field_in[:, 1], v_rows[:, 1])
        t_imag = product(form, field_in[:, 0], v_rows[:, 1]) + product(form, field_in[:, 1], v_rows[:, 0])
        t_real = rounded(t_real * live_mask)
        t_imag = rounded(t_imag * live_mask)
        back = 'kibr,kvbr->kvi'
        y_real = product(back, u_rows[:, 0], t_real) - product(back, u_rows[:, 1], t_imag)
        y_imag = product(back, u_rows[:, 0], t_imag) + product(back, u_rows[:, 1], t_real)
        return jnp.stack([y_real, y_imag], axis=1)

    rows_out = lax.map(one_row, jnp.arange(N_TROW, dtype=jnp.int32))
    return jnp.transpose(rows_out, (1, 2, 3, 0, 4)).reshape(NFQ, 2, NV, NR)


def adjoint_apply(field, u_tiles, v_tiles, rank_blocks):
    field_in = rounded(field).reshape(NFQ, 2, NV, N_TROW, TILE)

    def one_row(total, row_index):
        u_rows, v_rows, live_mask = row_factors(u_tiles, v_tiles, rank_blocks, row_index)
        row_field = lax.dynamic_index_in_dim(field_in, row_index, axis=3, keepdims=False)
        form = 'kvi,kibr->kvbr'
        s_real = product(form, row_field[:, 0], u_rows[:, 0]) + product(form, row_field[:, 1], u_rows[:, 1])
        s_imag = product(form, row_field[:, 1], u_rows[:, 0]) - product(form, row_field[:, 0], u_rows[:, 1])
        s_real = rounded(s_real * live_mask)
        s_imag = rounded(s_imag * live_mask)
        back = 'kvbr,krbj->kvbj'
        x_real = product(back, s_real, v_rows[:, 0]) + product(back, s_imag, v_rows[:, 1])
        x_imag = product(back, s_imag, v_rows[:, 0]) - product(back, s_real, v_rows[:, 1])
        return total + jnp.stack([x_real, x_imag], axis=1), None

    start_total = jnp.zeros((NFQ, 2, NV, N_TCOL, TILE), jnp.float32)
    total, unused = lax.scan(one_row, start_total, jnp.arange(N_TROW, dtype=jnp.int32))
    return total.reshape(NFQ, 2, NV, NS)


def reference(start_field, u_tiles, v_tiles, rank_blocks, onset_receiver, onset_source, omega):
    plus_field = start_field
    minus_field = jnp.zeros((NFQ, 2, NV, NR), jnp.float32)
    for iteration in range(ITERS):
        minus_field = rounded(window_field(forward_apply(plus_field, u_tiles, v_tiles, rank_blocks), onset_receiver, omega))
        plus_field = start_field - window_field(adjoint_apply(minus_field, u_tiles, v_tiles, rank_blocks), onset_source, omega)
    return plus_field, minus_field.astype(jnp.bfloat16)
```

```python
import functools

import jax
import jax.numpy as jnp
from jax import lax
from jax.experimental import pallas as pl
from jax.experimental.pallas import tpu as pltpu
from jax.sharding import PartitionSpec as P

RBLK = 256
NT = 1024
MESH = pl.DeviceIdType.MESH
F32 = jnp.float32
BF16 = jnp.bfloat16


def contract_last(left_side, right_side):
    return lax.dot_general(
        left_side, right_side, (((1,), (1,)), ((), ())), preferred_element_type=F32
    )


def contract_inner(left_side, right_side):
    return lax.dot_general(
        left_side, right_side, (((1,), (0,)), ((), ())), preferred_element_type=F32
    )


def sin_cos(angle):
    turns = jnp.floor(angle * 0.6366197723675814 + 0.5)
    rest = angle - turns * 1.5703125
    rest = rest - turns * 4.837512969970703e-4
    rest = rest - turns * 7.549789948768648e-8
    square = rest * rest
    sine = rest + rest * square * (
        -1.6666654611e-1 + square * (8.3321608736e-3 - square * 1.9515295891e-4)
    )
    cosine = 1.0 - 0.5 * square + square * square * (
        4.166664568298827e-2 + square * (-1.388731625493765e-3 + square * 2.443315711809948e-5)
    )
    quarter = turns - 4.0 * jnp.floor(turns * 0.25)
    swap = (quarter == 1.0) | (quarter == 3.0)
    first = jnp.where(swap, cosine, sine)
    second = jnp.where(swap, sine, cosine)
    first = jnp.where(quarter >= 2.0, -first, first)
    second = jnp.where((quarter == 1.0) | (quarter == 2.0), -second, second)
    return first, second


def prefix_sums(phi, count):
    sine, cosine = sin_cos(phi)
    sine_n, cosine_n = sin_cos(count * phi)
    still = phi == 0.0
    ratio = jnp.where(still, count, sine_n / jnp.where(still, 1.0, sine))
    cos_sum = ratio * (cosine_n * cosine + sine_n * sine)
    sin_sum = ratio * (sine_n * cosine - cosine_n * sine)
    return cos_sum, sin_sum


def gram(onset, omega_a, omega_b):
    count = onset.astype(F32)
    omega_a = jnp.full(count.shape, omega_a, F32)
    omega_b = jnp.full(count.shape, omega_b, F32)
    cos_aa, sin_aa = prefix_sums(omega_a, count)
    cos_bb, sin_bb = prefix_sums(omega_b, count)
    cos_sum, sin_sum = prefix_sums(0.5 * (omega_a + omega_b), count)
    cos_dif, sin_dif = prefix_sums(0.5 * (omega_a - omega_b), count)
    scale = 1.0 / NT
    g = {}
    g[0, 0] = scale * (count + cos_aa)
    g[1, 1] = scale * (count - cos_aa)
    g[0, 1] = -scale * sin_aa
    g[2, 2] = scale * (count + cos_bb)
    g[3, 3] = scale * (count - cos_bb)
    g[2, 3] = -scale * sin_bb
    g[0, 2] = scale * (cos_dif + cos_sum)
    g[1, 3] = scale * (cos_dif - cos_sum)
    g[0, 3] = -scale * (sin_sum - sin_dif)
    g[1, 2] = -scale * (sin_sum + sin_dif)
    for m in range(4):
        for n in range(m):
            g[m, n] = g[n, m]
    return g


def apply_gram(g, y):
    return [
        g[m, 0] * y[0] + g[m, 1] * y[1] + g[m, 2] * y[2] + g[m, 3] * y[3] for m in range(4)
    ]


def far_first(me, count):
    upper = me // max(count // 2, 1)
    upper = (upper + count - 1) // count
    order = []
    for step in range(count - 1):
        up = step + (step + count - me) // count
        high = count - 1 - step
        down = high - (me + count - high) // count
        order.append(upper * up + (1 - upper) * down)
    return order


def kernel(
    n_row, n_col,
    start_hbm, u_hbm, v_hbm, rank_ref, onset_r_hbm, onset_s_hbm, omega_hbm,
    plus_ref, minus_ref,
    start_buf, u_buf, v_buf, omega_ref, onset_buf, gram_buf,
    recv1, hand1, back1, recv2, hand2, back2,
    local_sem, ssem, rsem,
):
    row = lax.axis_index("trow")
    col = lax.axis_index("tcol")
    freq = lax.axis_index("tm")
    me_r, me_s = col * 2 + freq, row * 2 + freq

    copies = [
        pltpu.make_async_copy(source, target, local_sem.at[place])
        for place, source, target in (
            (0, omega_hbm, omega_ref),
            (1, start_hbm.at[0], start_buf),
            (2, onset_r_hbm, onset_buf.at[0]),
            (2, onset_s_hbm, onset_buf.at[1]),
            (3, v_hbm.at[0], v_buf),
            (4, u_hbm.at[0], u_buf),
        )
    ]
    for copy in copies:
        copy.start()

    def await_all(ref, sem):
        pltpu.make_async_copy(ref, ref, sem).wait()

    hubs_r = [{"tcol": place, "tm": 1} for place in far_first(col, n_col)]
    hubs_s = [{"trow": place, "tm": 1} for place in far_first(row, n_row)]
    barrier = pltpu.get_barrier_semaphore()

    def signal(device):
        pl.semaphore_signal(barrier, inc=1, device_id=device, device_id_type=MESH)

    @pl.when(freq == 1)
    def _():
        for device in hubs_r + hubs_s:
            signal(device)
            signal({**device, "tm": 0})

    signal({"tm": 1 - freq})

    def push(source, target, sem, device):
        pltpu.make_async_remote_copy(
            src_ref=source, dst_ref=target, send_sem=ssem, recv_sem=rsem.at[sem],
            device_id=device, device_id_type=MESH,
        ).start()

    def to_hubs(recv, me, sem, hubs, field):
        recv[me] = field.astype(BF16)
        for device in hubs:
            push(recv.at[me], recv.at[me], sem, device)

        @pl.when(freq == 0)
        def _():
            push(recv.at[me], recv.at[me], sem, {"tm": 1})

    def gather(recv, sem, gram):
        count = recv.shape[0]
        await_all(recv.at[pl.ds(0, count - 1)], rsem.at[sem])
        parts = []
        for k in range(2):
            total = recv[k].astype(F32)
            for index in range(k + 2, count, 2):
                total = total + recv[index].astype(F32)
            parts += [total[:8], total[8:]]
        done = apply_gram(gram, parts)
        return [jnp.concatenate([done[2 * k], done[2 * k + 1]], axis=0) for k in range(2)]

    entries = [(m, n) for m in range(4) for n in range(m, 4)]

    def kept_gram(side):
        g = {}
        for place, (m, n) in enumerate(entries):
            g[m, n] = g[n, m] = gram_buf[side, place]
        return g

    copies[0].wait()
    await_all(onset_buf, local_sem.at[2])

    @pl.when(freq == 1)
    def _():
        for side in range(2):
            g = gram(onset_buf[side], omega_ref[0], omega_ref[1])
            for place, entry in enumerate(entries):
                gram_buf[side, place] = g[entry]

    copies[1].wait()
    rows_in = jnp.concatenate([start_buf[0], start_buf[1]], axis=0).astype(BF16)
    copies[4].wait()
    first_real = contract_last(rows_in, v_buf[0])
    first_imag = contract_last(rows_in, v_buf[1])
    lane = lax.broadcasted_iota(jnp.int32, (8, first_real.shape[1]), 1)
    keep = lane < rank_ref[0, 0, 0] * RBLK
    t_real = jnp.where(keep, first_real[:8] - first_imag[8:], 0.0)
    t_imag = jnp.where(keep, first_imag[:8] + first_real[8:], 0.0)
    packed = jnp.concatenate([t_real, t_imag], axis=0).astype(BF16)

    copies[5].wait()
    second_real = contract_last(packed, u_buf[0])
    second_imag = contract_last(packed, u_buf[1])
    field = jnp.concatenate(
        [second_real[:8] - second_imag[8:], second_imag[:8] + second_real[8:]], axis=0
    )
    pl.semaphore_wait(barrier, n_row + n_col - 1)
    to_hubs(recv1, me_r, 0, hubs_r, field)

    @pl.when(freq == 1)
    def _():
        done = gather(recv1, 0, kept_gram(0))
        hand1[...] = done[0].astype(BF16)
        push(hand1, back1, 2, {"tm": 0})
        back1[...] = done[1].astype(BF16)

    @pl.when(freq == 0)
    def _():
        await_all(back1, rsem.at[2])

    rows_back = back1[...]
    first_real = contract_inner(rows_back, u_buf[0])
    first_imag = contract_inner(rows_back, u_buf[1])
    s_real = jnp.where(keep, first_real[:8] + first_imag[8:], 0.0)
    s_imag = jnp.where(keep, first_real[8:] - first_imag[:8], 0.0)
    packed_back = jnp.concatenate([s_real, s_imag], axis=0).astype(BF16)
    second_real = contract_inner(packed_back, v_buf[0])
    second_imag = contract_inner(packed_back, v_buf[1])
    field = jnp.concatenate(
        [second_real[:8] + second_imag[8:], second_real[8:] - second_imag[:8]], axis=0
    )
    to_hubs(recv2, me_s, 1, hubs_s, field)
    minus_ref[0, 0] = rows_back[:8]
    minus_ref[0, 1] = rows_back[8:]

    @pl.when(freq == 1)
    def _():
        done = gather(recv2, 1, kept_gram(1))
        hand2[...] = done[0].astype(BF16)
        push(hand2, back2, 3, {"tm": 0})
        back2[...] = done[1].astype(BF16)

    @pl.when(freq == 0)
    def _():
        await_all(back2, rsem.at[3])

    last = back2[...].astype(F32)
    plus_ref[0, 0] = start_buf[0] - last[:8]
    plus_ref[0, 1] = start_buf[1] - last[8:]
    await_all(recv1.at[pl.ds(0, n_col)], ssem)
    await_all(recv2.at[pl.ds(0, n_row)], ssem)


def epilogue(plus_ref, minus_ref, plus_out, minus_out, sem):
    copies = [
        pltpu.make_async_copy(plus_ref, plus_out, sem.at[0]),
        pltpu.make_async_copy(minus_ref, minus_out, sem.at[1]),
    ]
    for copy in copies:
        copy.start()
    for copy in copies:
        copy.wait()


def per_device(start_field, u_tiles, v_tiles, rank_blocks, onset_receiver, onset_source, omega):
    n_row = lax.axis_size("trow")
    n_col = lax.axis_size("tcol")
    tile_r, tile_s = u_tiles.shape[2], v_tiles.shape[3]
    hbm = pl.BlockSpec(memory_space=pl.ANY)
    vmem = pl.BlockSpec(memory_space=pltpu.VMEM)
    sems = pltpu.SemaphoreType.DMA
    shapes = (
        jax.ShapeDtypeStruct((1, 2, 8, tile_s), F32),
        jax.ShapeDtypeStruct((1, 2, 8, tile_r), BF16),
    )
    plus, minus = pl.pallas_call(
        functools.partial(kernel, n_row, n_col),
        out_shape=shapes,
        in_specs=[hbm] * 3 + [pl.BlockSpec(memory_space=pltpu.SMEM)] + [hbm] * 3,
        out_specs=(vmem, vmem),
        scratch_shapes=[
            pltpu.VMEM(start_field.shape[1:], F32),
            pltpu.VMEM(u_tiles.shape[1:], BF16),
            pltpu.VMEM(v_tiles.shape[1:], BF16),
            pltpu.SMEM((2,), F32),
            pltpu.VMEM((2, 8, tile_r), jnp.int32),
            pltpu.VMEM((2, 10, 8, tile_r), F32),
            pltpu.VMEM((2 * n_col, 16, tile_r), BF16),
            pltpu.VMEM((16, tile_r), BF16),
            pltpu.VMEM((16, tile_r), BF16),
            pltpu.VMEM((2 * n_row, 16, tile_s), BF16),
            pltpu.VMEM((16, tile_s), BF16),
            pltpu.VMEM((16, tile_s), BF16),
            sems((5,)),
            sems(()),
            sems((4,)),
        ],
        compiler_params=pltpu.CompilerParams(
            collective_id=0, has_side_effects=True, vmem_limit_bytes=24 * 1024 * 1024
        ),
    )(
        pin(start_field), pin(u_tiles), pin(v_tiles), rank_blocks,
        pin(onset_receiver), pin(onset_source), pin(omega),
    )
    return pl.pallas_call(
        epilogue,
        out_shape=shapes,
        in_specs=[vmem, vmem],
        out_specs=(pl.BlockSpec(memory_space=pltpu.HBM),) * 2,
        scratch_shapes=[sems((2,))],
    )(
        pltpu.with_memory_space_constraint(plus, pltpu.VMEM),
        pltpu.with_memory_space_constraint(minus, pltpu.VMEM),
    )


def pin(x):
    return pltpu.with_memory_space_constraint(x, pltpu.MemorySpace.HBM)


def solution(mesh):
    placed = (
        P("tm", None, None, "tcol"),
        P("tm", None, "trow", "tcol"),
        P("tm", None, "trow", "tcol"),
        P("tm", "trow", "tcol"),
        P(None, "trow"),
        P(None, "tcol"),
        P(),
    )
    return jax.shard_map(
        per_device,
        mesh=mesh,
        in_specs=placed,
        out_specs=(P("tm", None, None, "tcol"), P("tm", None, None, "trow")),
        check_vma=False,
    )
```

```python
import functools

import jax
import jax.numpy as jnp
from jax import lax
from jax.experimental import pallas as pl
from jax.experimental.pallas import tpu as pltpu
from jax.sharding import PartitionSpec as P

RBLK = 256
NT = 1024
MESH = pl.DeviceIdType.MESH
F32 = jnp.float32
BF16 = jnp.bfloat16


def contract_last(left_side, right_side):
    return lax.dot_general(
        left_side, right_side, (((1,), (1,)), ((), ())), preferred_element_type=F32
    )


def contract_inner(left_side, right_side):
    return lax.dot_general(
        left_side, right_side, (((1,), (0,)), ((), ())), preferred_element_type=F32
    )


def sin_cos(angle):
    turns = jnp.floor(angle * 0.6366197723675814 + 0.5)
    rest = angle - turns * 1.5703125
    rest = rest - turns * 4.837512969970703e-4
    rest = rest - turns * 7.549789948768648e-8
    square = rest * rest
    sine = rest + rest * square * (
        -1.6666654611e-1 + square * (8.3321608736e-3 - square * 1.9515295891e-4)
    )
    cosine = 1.0 - 0.5 * square + square * square * (
        4.166664568298827e-2 + square * (-1.388731625493765e-3 + square * 2.443315711809948e-5)
    )
    quarter = turns - 4.0 * jnp.floor(turns * 0.25)
    swap = (quarter == 1.0) | (quarter == 3.0)
    first = jnp.where(swap, cosine, sine)
    second = jnp.where(swap, sine, cosine)
    first = jnp.where(quarter >= 2.0, -first, first)
    second = jnp.where((quarter == 1.0) | (quarter == 2.0), -second, second)
    return first, second


def prefix_sums(phi, count):
    sine, cosine = sin_cos(phi)
    sine_n, cosine_n = sin_cos(count * phi)
    still = phi == 0.0
    ratio = jnp.where(still, count, sine_n / jnp.where(still, 1.0, sine))
    cos_sum = ratio * (cosine_n * cosine + sine_n * sine)
    sin_sum = ratio * (sine_n * cosine - cosine_n * sine)
    return cos_sum, sin_sum


def gram(onset, omega_a, omega_b):
    count = onset.astype(F32)
    omega_a = jnp.full(count.shape, omega_a, F32)
    omega_b = jnp.full(count.shape, omega_b, F32)
    cos_aa, sin_aa = prefix_sums(omega_a, count)
    cos_bb, sin_bb = prefix_sums(omega_b, count)
    cos_sum, sin_sum = prefix_sums(0.5 * (omega_a + omega_b), count)
    cos_dif, sin_dif = prefix_sums(0.5 * (omega_a - omega_b), count)
    scale = 1.0 / NT
    g = {}
    g[0, 0] = scale * (count + cos_aa)
    g[1, 1] = scale * (count - cos_aa)
    g[0, 1] = -scale * sin_aa
    g[2, 2] = scale * (count + cos_bb)
    g[3, 3] = scale * (count - cos_bb)
    g[2, 3] = -scale * sin_bb
    g[0, 2] = scale * (cos_dif + cos_sum)
    g[1, 3] = scale * (cos_dif - cos_sum)
    g[0, 3] = -scale * (sin_sum - sin_dif)
    g[1, 2] = -scale * (sin_sum + sin_dif)
    for m in range(4):
        for n in range(m):
            g[m, n] = g[n, m]
    return g


def apply_gram(g, y):
    return [
        g[m, 0] * y[0] + g[m, 1] * y[1] + g[m, 2] * y[2] + g[m, 3] * y[3] for m in range(4)
    ]


def far_first(me, count):
    upper = me // max(count // 2, 1)
    upper = (upper + count - 1) // count
    order = []
    for step in range(count - 1):
        up = step + (step + count - me) // count
        high = count - 1 - step
        down = high - (me + count - high) // count
        order.append(upper * up + (1 - upper) * down)
    return order


def kernel(
    n_row, n_col,
    start_hbm, u_hbm, v_hbm, rank_ref, onset_r_hbm, onset_s_hbm, omega_hbm,
    plus_ref, minus_ref,
    start_buf, u_buf, v_buf, omega_ref, onset_buf, gram_buf,
    recv1, hand1, back1, recv2, hand2, back2,
    local_sem, ssem, rsem,
):
    row = lax.axis_index("trow")
    col = lax.axis_index("tcol")
    freq = lax.axis_index("tm")
    me_r, me_s = col * 2 + freq, row * 2 + freq
    half = u_buf.shape[1] // 2

    copies = [
        pltpu.make_async_copy(source, target, local_sem.at[place])
        for place, source, target in (
            (0, omega_hbm, omega_ref),
            (1, start_hbm.at[0], start_buf),
            (2, onset_r_hbm, onset_buf.at[0]),
            (2, onset_s_hbm, onset_buf.at[1]),
            (3, v_hbm.at[0, 0], v_buf.at[0]),
            (4, v_hbm.at[0, 1], v_buf.at[1]),
            (5, u_hbm.at[0, :, pl.ds(0, half)], u_buf.at[:, pl.ds(0, half)]),
            (6, u_hbm.at[0, :, pl.ds(half, half)], u_buf.at[:, pl.ds(half, half)]),
        )
    ]
    for copy in copies:
        copy.start()

    def await_all(ref, sem):
        pltpu.make_async_copy(ref, ref, sem).wait()

    hubs_r = [{"tcol": place, "tm": 1} for place in far_first(col, n_col)]
    hubs_s = [{"trow": place, "tm": 1} for place in far_first(row, n_row)]
    barrier = pltpu.get_barrier_semaphore()

    def signal(device):
        pl.semaphore_signal(barrier, inc=1, device_id=device, device_id_type=MESH)

    @pl.when(freq == 1)
    def _():
        for device in hubs_r + hubs_s:
            signal(device)
            signal({**device, "tm": 0})

    @pl.when(freq == 0)
    def _():
        for device in hubs_s:
            signal({**device, "tm": 0})

    signal({"tm": 1 - freq})

    def push(source, target, sem, device):
        pltpu.make_async_remote_copy(
            src_ref=source, dst_ref=target, send_sem=ssem, recv_sem=rsem.at[sem],
            device_id=device, device_id_type=MESH,
        ).start()

    def add(recv, places):
        total = recv[places[0]].astype(F32)
        for place in places[1:]:
            total = total + recv[place].astype(F32)
        return [total[:8], total[8:]]

    entries = [(m, n) for m in range(4) for n in range(m, 4)]

    def kept_gram(side):
        g = {}
        for place, (m, n) in enumerate(entries):
            g[m, n] = g[n, m] = gram_buf[side, place]
        return g

    copies[0].wait()
    await_all(onset_buf, local_sem.at[2])

    for side in range(2):
        g = gram(onset_buf[side], omega_ref[0], omega_ref[1])
        for place, entry in enumerate(entries):
            gram_buf[side, place] = g[entry]

    copies[1].wait()
    rows_in = jnp.concatenate([start_buf[0], start_buf[1]], axis=0).astype(BF16)
    copies[4].wait()
    first_real = contract_last(rows_in, v_buf[0])
    copies[5].wait()
    first_imag = contract_last(rows_in, v_buf[1])
    lane = lax.broadcasted_iota(jnp.int32, (8, first_real.shape[1]), 1)
    keep = lane < rank_ref[0, 0, 0] * RBLK
    t_real = jnp.where(keep, first_real[:8] - first_imag[8:], 0.0)
    t_imag = jnp.where(keep, first_imag[:8] + first_real[8:], 0.0)
    packed = jnp.concatenate([t_real, t_imag], axis=0).astype(BF16)

    for part in range(2):
        span = pl.ds(part * half, half)
        copies[6 + part].wait()
        second_real = contract_last(packed, u_buf[0, span])
        second_imag = contract_last(packed, u_buf[1, span])
        recv1[me_r, :, span] = jnp.concatenate(
            [second_real[:8] - second_imag[8:], second_imag[:8] + second_real[8:]], axis=0
        ).astype(BF16)
    pl.semaphore_wait(barrier, n_row + n_col - 1 + (1 - freq) * (n_row - 1))
    for device in hubs_r:
        push(recv1.at[me_r], recv1.at[me_r], 0, device)

    @pl.when(freq == 0)
    def _():
        push(recv1.at[me_r], recv1.at[me_r], 0, {"tm": 1})
        await_all(back1, rsem.at[1])

    @pl.when(freq == 1)
    def _():
        await_all(recv1.at[pl.ds(0, 2 * n_col - 1)], rsem.at[0])
        parts = [add(recv1, range(k, 2 * n_col, 2)) for k in range(2)]
        done = apply_gram(kept_gram(0), parts[0] + parts[1])
        hand1[...] = jnp.concatenate(done[:2], axis=0).astype(BF16)
        push(hand1, back1, 1, {"tm": 0})
        back1[...] = jnp.concatenate(done[2:], axis=0).astype(BF16)

    rows_back = back1[...]
    first_real = contract_inner(rows_back, u_buf[0])
    first_imag = contract_inner(rows_back, u_buf[1])
    s_real = jnp.where(keep, first_real[:8] + first_imag[8:], 0.0)
    s_imag = jnp.where(keep, first_real[8:] - first_imag[:8], 0.0)
    packed_back = jnp.concatenate([s_real, s_imag], axis=0).astype(BF16)
    second_real = contract_inner(packed_back, v_buf[0])
    second_imag = contract_inner(packed_back, v_buf[1])
    recv2[me_s] = jnp.concatenate(
        [second_real[:8] + second_imag[8:], second_real[8:] - second_imag[:8]], axis=0
    ).astype(BF16)
    own = [2 * place for place in range(n_row)]
    far = [2 * place + 1 for place in range(n_row)]

    @pl.when(freq == 0)
    def _():
        for tm in (0, 1):
            for device in hubs_s:
                push(recv2.at[me_s], recv2.at[me_s], 2, {**device, "tm": tm})
        push(recv2.at[me_s], recv2.at[me_s], 2, {"tm": 1})
        minus_ref[0, 0] = rows_back[:8]
        minus_ref[0, 1] = rows_back[8:]
        await_all(hand2, rsem.at[3])
        await_all(recv2.at[pl.ds(0, n_row - 1)], rsem.at[2])
        g, y = kept_gram(1), add(recv2, own)
        for m in range(2):
            last = hand2[8 * m : 8 * m + 8].astype(F32)
            plus_ref[0, m] = start_buf[m] - (g[m, 0] * y[0] + g[m, 1] * y[1] + last)

    @pl.when(freq == 1)
    def _():
        for device in hubs_s:
            push(recv2.at[me_s], recv2.at[me_s], 3, device)
        minus_ref[0, 0] = rows_back[:8]
        minus_ref[0, 1] = rows_back[8:]
        await_all(recv2.at[pl.ds(0, n_row - 1)], rsem.at[3])
        g, y = kept_gram(1), add(recv2, far)
        back2[...] = jnp.concatenate(
            [g[m, 2] * y[0] + g[m, 3] * y[1] for m in range(2)], axis=0
        ).astype(BF16)
        push(back2, hand2, 3, {"tm": 0})
        await_all(recv2.at[pl.ds(0, n_row)], rsem.at[2])
        x = add(recv2, own)
        done = apply_gram(g, x + y)
        for m in range(2):
            plus_ref[0, m] = start_buf[m] - done[2 + m]

    await_all(recv1.at[pl.ds(0, n_col)], ssem)
    await_all(recv2.at[pl.ds(0, n_row)], ssem)

    @pl.when(freq == 0)
    def _():
        await_all(recv2.at[pl.ds(0, n_row - 1)], ssem)


def epilogue(plus_ref, minus_ref, plus_out, minus_out, sem):
    copies = [
        pltpu.make_async_copy(plus_ref, plus_out, sem.at[0]),
        pltpu.make_async_copy(minus_ref, minus_out, sem.at[1]),
    ]
    for copy in copies:
        copy.start()
    for copy in copies:
        copy.wait()


def per_device(start_field, u_tiles, v_tiles, rank_blocks, onset_receiver, onset_source, omega):
    n_row = lax.axis_size("trow")
    n_col = lax.axis_size("tcol")
    tile_r, tile_s = u_tiles.shape[2], v_tiles.shape[3]
    hbm = pl.BlockSpec(memory_space=pl.ANY)
    vmem = pl.BlockSpec(memory_space=pltpu.VMEM)
    sems = pltpu.SemaphoreType.DMA
    shapes = (
        jax.ShapeDtypeStruct((1, 2, 8, tile_s), F32),
        jax.ShapeDtypeStruct((1, 2, 8, tile_r), BF16),
    )
    plus, minus = pl.pallas_call(
        functools.partial(kernel, n_row, n_col),
        out_shape=shapes,
        in_specs=[hbm] * 3 + [pl.BlockSpec(memory_space=pltpu.SMEM)] + [hbm] * 3,
        out_specs=(vmem, vmem),
        scratch_shapes=[
            pltpu.VMEM(start_field.shape[1:], F32),
            pltpu.VMEM(u_tiles.shape[1:], BF16),
            pltpu.VMEM(v_tiles.shape[1:], BF16),
            pltpu.SMEM((2,), F32),
            pltpu.VMEM((2, 8, tile_r), jnp.int32),
            pltpu.VMEM((2, 10, 8, tile_r), F32),
            pltpu.VMEM((2 * n_col, 16, tile_r), BF16),
            pltpu.VMEM((16, tile_r), BF16),
            pltpu.VMEM((16, tile_r), BF16),
            pltpu.VMEM((2 * n_row, 16, tile_s), BF16),
            pltpu.VMEM((16, tile_s), BF16),
            pltpu.VMEM((16, tile_s), BF16),
            sems((7,)),
            sems(()),
            sems((4,)),
        ],
        compiler_params=pltpu.CompilerParams(
            collective_id=0, has_side_effects=True, vmem_limit_bytes=24 * 1024 * 1024
        ),
    )(
        pin(start_field), pin(u_tiles), pin(v_tiles), rank_blocks,
        pin(onset_receiver), pin(onset_source), pin(omega),
    )
    return pl.pallas_call(
        epilogue,
        out_shape=shapes,
        in_specs=[vmem, vmem],
        out_specs=(pl.BlockSpec(memory_space=pltpu.HBM),) * 2,
        scratch_shapes=[sems((2,))],
    )(
        pltpu.with_memory_space_constraint(plus, pltpu.VMEM),
        pltpu.with_memory_space_constraint(minus, pltpu.VMEM),
    )


def pin(x):
    return pltpu.with_memory_space_constraint(x, pltpu.MemorySpace.HBM)


def solution(mesh):
    placed = (
        P("tm", None, None, "tcol"),
        P("tm", None, "trow", "tcol"),
        P("tm", None, "trow", "tcol"),
        P("tm", "trow", "tcol"),
        P(None, "trow"),
        P(None, "tcol"),
        P(),
    )
    return jax.shard_map(
        per_device,
        mesh=mesh,
        in_specs=placed,
        out_specs=(P("tm", None, None, "tcol"), P("tm", None, None, "trow")),
        check_vma=False,
    )
```

```python
import functools

import jax
import jax.numpy as jnp
from jax import lax
from jax.experimental import pallas as pl
from jax.experimental.pallas import tpu as pltpu
from jax.sharding import PartitionSpec as P

RBLK = 256
NT = 1024
MESH = pl.DeviceIdType.MESH
F32 = jnp.float32
BF16 = jnp.bfloat16


def contract_last(left_side, right_side):
    return lax.dot_general(
        left_side, right_side, (((1,), (1,)), ((), ())), preferred_element_type=F32
    )


def contract_inner(left_side, right_side):
    return lax.dot_general(
        left_side, right_side, (((1,), (0,)), ((), ())), preferred_element_type=F32
    )


def sin_cos(angle):
    turns = jnp.floor(angle * 0.6366197723675814 + 0.5)
    rest = angle - turns * 1.5703125
    rest = rest - turns * 4.837512969970703e-4
    rest = rest - turns * 7.549789948768648e-8
    square = rest * rest
    sine = rest + rest * square * (
        -1.6666654611e-1 + square * (8.3321608736e-3 - square * 1.9515295891e-4)
    )
    cosine = 1.0 - 0.5 * square + square * square * (
        4.166664568298827e-2 + square * (-1.388731625493765e-3 + square * 2.443315711809948e-5)
    )
    quarter = turns - 4.0 * jnp.floor(turns * 0.25)
    swap = (quarter == 1.0) | (quarter == 3.0)
    first = jnp.where(swap, cosine, sine)
    second = jnp.where(swap, sine, cosine)
    first = jnp.where(quarter >= 2.0, -first, first)
    second = jnp.where((quarter == 1.0) | (quarter == 2.0), -second, second)
    return first, second


def prefix_sums(phi, count):
    sine, cosine = sin_cos(phi)
    sine_n, cosine_n = sin_cos(count * phi)
    still = phi == 0.0
    ratio = jnp.where(still, count, sine_n / jnp.where(still, 1.0, sine))
    cos_sum = ratio * (cosine_n * cosine + sine_n * sine)
    sin_sum = ratio * (sine_n * cosine - cosine_n * sine)
    return cos_sum, sin_sum


def gram(onset, omega_a, omega_b):
    count = onset.astype(F32)
    omega_a = jnp.full(count.shape, omega_a, F32)
    omega_b = jnp.full(count.shape, omega_b, F32)
    cos_aa, sin_aa = prefix_sums(omega_a, count)
    cos_bb, sin_bb = prefix_sums(omega_b, count)
    cos_sum, sin_sum = prefix_sums(0.5 * (omega_a + omega_b), count)
    cos_dif, sin_dif = prefix_sums(0.5 * (omega_a - omega_b), count)
    scale = 1.0 / NT
    g = {}
    g[0, 0] = scale * (count + cos_aa)
    g[1, 1] = scale * (count - cos_aa)
    g[0, 1] = -scale * sin_aa
    g[2, 2] = scale * (count + cos_bb)
    g[3, 3] = scale * (count - cos_bb)
    g[2, 3] = -scale * sin_bb
    g[0, 2] = scale * (cos_dif + cos_sum)
    g[1, 3] = scale * (cos_dif - cos_sum)
    g[0, 3] = -scale * (sin_sum - sin_dif)
    g[1, 2] = -scale * (sin_sum + sin_dif)
    for m in range(4):
        for n in range(m):
            g[m, n] = g[n, m]
    return g


def apply_gram(g, y):
    return [
        g[m, 0] * y[0] + g[m, 1] * y[1] + g[m, 2] * y[2] + g[m, 3] * y[3] for m in range(4)
    ]


def far_first(me, count):
    upper = me // max(count // 2, 1)
    upper = (upper + count - 1) // count
    order = []
    for step in range(count - 1):
        up = step + (step + count - me) // count
        high = count - 1 - step
        down = high - (me + count - high) // count
        order.append(upper * up + (1 - upper) * down)
    return order


def diagonal_first(me, count):
    line, spot = me // 2, me % 2
    lines = count // 2
    steps = [(up, 1) for up in range(1, lines)] + [(0, 1)] + [(up, 0) for up in range(1, lines)]
    return [(line + up) % lines * 2 + (spot + over) % 2 for up, over in steps]


def kernel(
    n_row, n_col,
    start_hbm, u_hbm, v_hbm, rank_ref, onset_r_hbm, onset_s_hbm, omega_hbm,
    plus_ref, minus_ref,
    start_buf, u_buf, v_buf, omega_ref, onset_buf, gram_buf,
    recv1, hand1, back1, recv2, hand2, back2,
    local_sem, ssem, rsem,
):
    row = lax.axis_index("trow")
    col = lax.axis_index("tcol")
    freq = lax.axis_index("tm")
    me_r, me_s = col * 2 + freq, row * 2 + freq
    half = u_buf.shape[1] // 2

    for place, source, target in (
        (0, start_hbm.at[0], start_buf),
        (0, v_hbm.at[0, 0], v_buf.at[0]),
        (4, v_hbm.at[0, 1], v_buf.at[1]),
        (1, omega_hbm, omega_ref),
        (2, u_hbm.at[0, :, pl.ds(0, half)], u_buf.at[:, pl.ds(0, half)]),
        (3, u_hbm.at[0, :, pl.ds(half, half)], u_buf.at[:, pl.ds(half, half)]),
        (1, onset_r_hbm, onset_buf.at[0]),
        (1, onset_s_hbm, onset_buf.at[1]),
    ):
        pltpu.make_async_copy(source, target, local_sem.at[place]).start()

    def await_all(ref, sem):
        pltpu.make_async_copy(ref, ref, sem).wait()

    hubs_r = [{"tcol": place, "tm": 1} for place in far_first(col, n_col)]
    hubs_s = [{"trow": place, "tm": 1} for place in diagonal_first(row, n_row)]
    barrier = pltpu.get_barrier_semaphore()

    def signal(device):
        pl.semaphore_signal(barrier, inc=1, device_id=device, device_id_type=MESH)

    @pl.when(freq == 1)
    def _():
        for device in hubs_r + hubs_s:
            signal(device)
            signal({**device, "tm": 0})

    @pl.when(freq == 0)
    def _():
        for device in hubs_s:
            signal({**device, "tm": 0})

    signal({"tm": 1 - freq})

    def push(source, target, sem, device):
        pltpu.make_async_remote_copy(
            src_ref=source, dst_ref=target, send_sem=ssem, recv_sem=rsem.at[sem],
            device_id=device, device_id_type=MESH,
        ).start()

    def add(recv, places):
        total = recv[places[0]].astype(F32)
        for place in places[1:]:
            total = total + recv[place].astype(F32)
        return [total[:8], total[8:]]

    entries = [(m, n) for m in range(4) for n in range(m, 4)]

    def kept_gram(side):
        g = {}
        for place, (m, n) in enumerate(entries):
            g[m, n] = g[n, m] = gram_buf[side, place]
        return g

    await_all(start_buf, local_sem.at[0])
    await_all(v_buf.at[0], local_sem.at[0])
    rows_in = jnp.concatenate([start_buf[0], start_buf[1]], axis=0).astype(BF16)
    first_real = contract_last(rows_in, v_buf[0])
    await_all(v_buf.at[1], local_sem.at[4])
    first_imag = contract_last(rows_in, v_buf[1])
    lane = lax.broadcasted_iota(jnp.int32, (8, first_real.shape[1]), 1)
    keep = lane < rank_ref[0, 0, 0] * RBLK
    t_real = jnp.where(keep, first_real[:8] - first_imag[8:], 0.0)
    t_imag = jnp.where(keep, first_imag[:8] + first_real[8:], 0.0)
    packed = jnp.concatenate([t_real, t_imag], axis=0).astype(BF16)

    for part in range(2):
        span = pl.ds(part * half, half)
        await_all(u_buf.at[:, span], local_sem.at[2 + part])
        second_real = contract_last(packed, u_buf[0, span])
        second_imag = contract_last(packed, u_buf[1, span])
        recv1[me_r, :, span] = jnp.concatenate(
            [second_real[:8] - second_imag[8:], second_imag[:8] + second_real[8:]], axis=0
        ).astype(BF16)
    await_all(onset_buf, local_sem.at[1])
    pltpu.make_async_copy(omega_hbm, omega_ref, local_sem.at[1]).wait()
    pl.semaphore_wait(barrier, n_row + n_col - 1 + (1 - freq) * (n_row - 1))

    @pl.when(freq == 0)
    def _():
        for device in hubs_r + [{"tm": 1}]:
            push(recv1.at[me_r], recv1.at[me_r], 0, device)

    @pl.when(freq == 1)
    def _():
        for device in hubs_r:
            push(recv1.at[me_r], recv1.at[me_r], 3, device)

    for side in range(2):
        g = gram(onset_buf[side], omega_ref[0], omega_ref[1])
        for place, entry in enumerate(entries):
            gram_buf[side, place] = g[entry]

    @pl.when(freq == 0)
    def _():
        await_all(back1, rsem.at[0])

    @pl.when(freq == 1)
    def _():
        g = kept_gram(0)
        await_all(recv1.at[pl.ds(0, n_col - 1)], rsem.at[3])
        near = add(recv1, range(1, 2 * n_col, 2))
        near = [g[m, 2] * near[0] + g[m, 3] * near[1] for m in range(4)]
        await_all(recv1.at[pl.ds(0, n_col)], rsem.at[0])
        y = add(recv1, range(0, 2 * n_col, 2))
        for m in range(2):
            hand1[8 * m : 8 * m + 8] = (g[m, 0] * y[0] + g[m, 1] * y[1] + near[m]).astype(BF16)
        push(hand1, back1, 0, {"tm": 0})
        back1[...] = jnp.concatenate(
            [g[m, 0] * y[0] + g[m, 1] * y[1] + near[m] for m in (2, 3)], axis=0
        ).astype(BF16)

    rows_back = back1[...]
    first_real = contract_inner(rows_back, u_buf[0])
    first_imag = contract_inner(rows_back, u_buf[1])
    s_real = jnp.where(keep, first_real[:8] + first_imag[8:], 0.0)
    s_imag = jnp.where(keep, first_real[8:] - first_imag[:8], 0.0)
    packed_back = jnp.concatenate([s_real, s_imag], axis=0).astype(BF16)
    second_real = contract_inner(packed_back, v_buf[0])
    second_imag = contract_inner(packed_back, v_buf[1])
    recv2[me_s] = jnp.concatenate(
        [second_real[:8] + second_imag[8:], second_real[8:] - second_imag[:8]], axis=0
    ).astype(BF16)
    own = [2 * place for place in range(n_row)]
    far = [2 * place + 1 for place in range(n_row)]

    @pl.when(freq == 0)
    def _():
        for tm in (0, 1):
            for device in hubs_s:
                push(recv2.at[me_s], recv2.at[me_s], 1, {**device, "tm": tm})
        push(recv2.at[me_s], recv2.at[me_s], 1, {"tm": 1})
        minus_ref[0, 0] = rows_back[:8]
        minus_ref[0, 1] = rows_back[8:]
        await_all(hand2, rsem.at[2])
        await_all(recv2.at[pl.ds(0, n_row - 1)], rsem.at[1])
        g, y = kept_gram(1), add(recv2, own)
        for m in range(2):
            last = hand2[8 * m : 8 * m + 8].astype(F32)
            plus_ref[0, m] = start_buf[m] - (g[m, 0] * y[0] + g[m, 1] * y[1] + last)

    @pl.when(freq == 1)
    def _():
        for device in hubs_s:
            push(recv2.at[me_s], recv2.at[me_s], 2, device)
        minus_ref[0, 0] = rows_back[:8]
        minus_ref[0, 1] = rows_back[8:]
        await_all(recv2.at[pl.ds(0, n_row - 1)], rsem.at[2])
        g, y = kept_gram(1), add(recv2, far)
        back2[...] = jnp.concatenate(
            [g[m, 2] * y[0] + g[m, 3] * y[1] for m in range(2)], axis=0
        ).astype(BF16)
        push(back2, hand2, 2, {"tm": 0})
        await_all(recv2.at[pl.ds(0, n_row)], rsem.at[1])
        x = add(recv2, own)
        done = apply_gram(g, x + y)
        for m in range(2):
            plus_ref[0, m] = start_buf[m] - done[2 + m]

    await_all(recv1.at[pl.ds(0, n_col)], ssem)
    await_all(recv2.at[pl.ds(0, n_row)], ssem)

    @pl.when(freq == 0)
    def _():
        await_all(recv2.at[pl.ds(0, n_row - 1)], ssem)


def epilogue(plus_ref, minus_ref, plus_out, minus_out, sem):
    copies = [
        pltpu.make_async_copy(plus_ref, plus_out, sem.at[0]),
        pltpu.make_async_copy(minus_ref, minus_out, sem.at[1]),
    ]
    for copy in copies:
        copy.start()
    for copy in copies:
        copy.wait()


def per_device(start_field, u_tiles, v_tiles, rank_blocks, onset_receiver, onset_source, omega):
    n_row = lax.axis_size("trow")
    n_col = lax.axis_size("tcol")
    tile_r, tile_s = u_tiles.shape[2], v_tiles.shape[3]
    hbm = pl.BlockSpec(memory_space=pl.ANY)
    vmem = pl.BlockSpec(memory_space=pltpu.VMEM)
    sems = pltpu.SemaphoreType.DMA
    shapes = (
        jax.ShapeDtypeStruct((1, 2, 8, tile_s), F32),
        jax.ShapeDtypeStruct((1, 2, 8, tile_r), BF16),
    )
    plus, minus = pl.pallas_call(
        functools.partial(kernel, n_row, n_col),
        out_shape=shapes,
        in_specs=[hbm] * 3 + [pl.BlockSpec(memory_space=pltpu.SMEM)] + [hbm] * 3,
        out_specs=(vmem, vmem),
        scratch_shapes=[
            pltpu.VMEM(start_field.shape[1:], F32),
            pltpu.VMEM(u_tiles.shape[1:], BF16),
            pltpu.VMEM(v_tiles.shape[1:], BF16),
            pltpu.SMEM((2,), F32),
            pltpu.VMEM((2, 8, tile_r), jnp.int32),
            pltpu.VMEM((2, 10, 8, tile_r), F32),
            pltpu.VMEM((2 * n_col, 16, tile_r), BF16),
            pltpu.VMEM((16, tile_r), BF16),
            pltpu.VMEM((16, tile_r), BF16),
            pltpu.VMEM((2 * n_row, 16, tile_s), BF16),
            pltpu.VMEM((16, tile_s), BF16),
            pltpu.VMEM((16, tile_s), BF16),
            sems((5,)),
            sems(()),
            sems((4,)),
        ],
        compiler_params=pltpu.CompilerParams(
            collective_id=0, has_side_effects=True, vmem_limit_bytes=24 * 1024 * 1024
        ),
    )(
        pin(start_field), pin(u_tiles), pin(v_tiles), rank_blocks,
        pin(onset_receiver), pin(onset_source), pin(omega),
    )
    return pl.pallas_call(
        epilogue,
        out_shape=shapes,
        in_specs=[vmem, vmem],
        out_specs=(pl.BlockSpec(memory_space=pltpu.HBM),) * 2,
        scratch_shapes=[sems((2,))],
    )(
        pltpu.with_memory_space_constraint(plus, pltpu.VMEM),
        pltpu.with_memory_space_constraint(minus, pltpu.VMEM),
    )


def pin(x):
    return pltpu.with_memory_space_constraint(x, pltpu.MemorySpace.HBM)


def solution(mesh):
    placed = (
        P("tm", None, None, "tcol"),
        P("tm", None, "trow", "tcol"),
        P("tm", None, "trow", "tcol"),
        P("tm", "trow", "tcol"),
        P(None, "trow"),
        P(None, "tcol"),
        P(),
    )
    return jax.shard_map(
        per_device,
        mesh=mesh,
        in_specs=placed,
        out_specs=(P("tm", None, None, "tcol"), P("tm", None, None, "trow")),
        check_vma=False,
    )
```

```python
import functools

import jax
import jax.numpy as jnp
from jax import lax
from jax.experimental import pallas as pl
from jax.experimental.pallas import tpu as pltpu
from jax.sharding import PartitionSpec as P

RBLK = 256
NT = 1024
MESH = pl.DeviceIdType.MESH
F32 = jnp.float32
BF16 = jnp.bfloat16


def contract_last(left_side, right_side):
    return lax.dot_general(
        left_side, right_side, (((1,), (1,)), ((), ())), preferred_element_type=F32
    )


def contract_inner(left_side, right_side):
    return lax.dot_general(
        left_side, right_side, (((1,), (0,)), ((), ())), preferred_element_type=F32
    )


def sin_cos(angle):
    turns = jnp.floor(angle * 0.6366197723675814 + 0.5)
    rest = angle - turns * 1.5703125
    rest = rest - turns * 4.837512969970703e-4
    rest = rest - turns * 7.549789948768648e-8
    square = rest * rest
    sine = rest + rest * square * (
        -1.6666654611e-1 + square * (8.3321608736e-3 - square * 1.9515295891e-4)
    )
    cosine = 1.0 - 0.5 * square + square * square * (
        4.166664568298827e-2 + square * (-1.388731625493765e-3 + square * 2.443315711809948e-5)
    )
    quarter = turns - 4.0 * jnp.floor(turns * 0.25)
    swap = (quarter == 1.0) | (quarter == 3.0)
    first = jnp.where(swap, cosine, sine)
    second = jnp.where(swap, sine, cosine)
    first = jnp.where(quarter >= 2.0, -first, first)
    second = jnp.where((quarter == 1.0) | (quarter == 2.0), -second, second)
    return first, second


def prefix_sums(phi, count):
    sine, cosine = sin_cos(phi)
    sine_n, cosine_n = sin_cos(count * phi)
    still = phi == 0.0
    ratio = jnp.where(still, count, sine_n / jnp.where(still, 1.0, sine))
    cos_sum = ratio * (cosine_n * cosine + sine_n * sine)
    sin_sum = ratio * (sine_n * cosine - cosine_n * sine)
    return cos_sum, sin_sum


def gram(onset, omega_a, omega_b):
    count = onset.astype(F32)
    omega_a = jnp.full(count.shape, omega_a, F32)
    omega_b = jnp.full(count.shape, omega_b, F32)
    cos_aa, sin_aa = prefix_sums(omega_a, count)
    cos_bb, sin_bb = prefix_sums(omega_b, count)
    cos_sum, sin_sum = prefix_sums(0.5 * (omega_a + omega_b), count)
    cos_dif, sin_dif = prefix_sums(0.5 * (omega_a - omega_b), count)
    scale = 1.0 / NT
    g = {}
    g[0, 0] = scale * (count + cos_aa)
    g[1, 1] = scale * (count - cos_aa)
    g[0, 1] = -scale * sin_aa
    g[2, 2] = scale * (count + cos_bb)
    g[3, 3] = scale * (count - cos_bb)
    g[2, 3] = -scale * sin_bb
    g[0, 2] = scale * (cos_dif + cos_sum)
    g[1, 3] = scale * (cos_dif - cos_sum)
    g[0, 3] = -scale * (sin_sum - sin_dif)
    g[1, 2] = -scale * (sin_sum + sin_dif)
    for m in range(4):
        for n in range(m):
            g[m, n] = g[n, m]
    return g


def apply_gram(g, y):
    return [
        g[m, 0] * y[0] + g[m, 1] * y[1] + g[m, 2] * y[2] + g[m, 3] * y[3] for m in range(4)
    ]


def from_zero(me, count):
    return [step + (step + count - me) // count for step in range(count - 1)]


def kernel(
    n_row, n_col,
    start_hbm, u_hbm, v_hbm, rank_ref, onset_r_hbm, onset_s_hbm, omega_hbm,
    plus_ref, minus_ref,
    start_buf, u_buf, v_buf, omega_ref, onset_buf, gram_buf,
    recv1, hand1, back1, recv2, hand2, back2,
    local_sem, ssem, rsem,
):
    row = lax.axis_index("trow")
    col = lax.axis_index("tcol")
    freq = lax.axis_index("tm")
    me_r, me_s = col * 2 + freq, row * 2 + freq
    half = u_buf.shape[1] // 2

    for place, source, target in (
        (0, start_hbm.at[0], start_buf),
        (0, v_hbm.at[0, 0], v_buf.at[0]),
        (4, v_hbm.at[0, 1], v_buf.at[1]),
        (1, omega_hbm, omega_ref),
        (2, u_hbm.at[0, :, pl.ds(0, half)], u_buf.at[:, pl.ds(0, half)]),
        (3, u_hbm.at[0, :, pl.ds(half, half)], u_buf.at[:, pl.ds(half, half)]),
        (1, onset_r_hbm, onset_buf.at[0]),
        (1, onset_s_hbm, onset_buf.at[1]),
    ):
        pltpu.make_async_copy(source, target, local_sem.at[place]).start()

    def await_all(ref, sem):
        pltpu.make_async_copy(ref, ref, sem).wait()

    hubs_r = [{"tcol": place, "tm": 1} for place in from_zero(col, n_col)]
    hubs_s = [{"trow": place, "tm": 1} for place in from_zero(row, n_row)]
    barrier = pltpu.get_barrier_semaphore()

    def signal(device):
        pl.semaphore_signal(barrier, inc=1, device_id=device, device_id_type=MESH)

    @pl.when(freq == 1)
    def _():
        for device in hubs_r + hubs_s:
            signal(device)
            signal({**device, "tm": 0})

    @pl.when(freq == 0)
    def _():
        for device in hubs_s:
            signal({**device, "tm": 0})

    signal({"tm": 1 - freq})

    def push(source, target, sem, device):
        pltpu.make_async_remote_copy(
            src_ref=source, dst_ref=target, send_sem=ssem, recv_sem=rsem.at[sem],
            device_id=device, device_id_type=MESH,
        ).start()

    def add(recv, places):
        total = recv[places[0]].astype(F32)
        for place in places[1:]:
            total = total + recv[place].astype(F32)
        return [total[:8], total[8:]]

    entries = [(m, n) for m in range(4) for n in range(m, 4)]

    def kept_gram(side):
        g = {}
        for place, (m, n) in enumerate(entries):
            g[m, n] = g[n, m] = gram_buf[side, place]
        return g

    await_all(start_buf, local_sem.at[0])
    await_all(v_buf.at[0], local_sem.at[0])
    rows_in = jnp.concatenate([start_buf[0], start_buf[1]], axis=0).astype(BF16)
    first_real = contract_last(rows_in, v_buf[0])
    await_all(v_buf.at[1], local_sem.at[4])
    first_imag = contract_last(rows_in, v_buf[1])
    lane = lax.broadcasted_iota(jnp.int32, (8, first_real.shape[1]), 1)
    keep = lane < rank_ref[0, 0, 0] * RBLK
    t_real = jnp.where(keep, first_real[:8] - first_imag[8:], 0.0)
    t_imag = jnp.where(keep, first_imag[:8] + first_real[8:], 0.0)
    packed = jnp.concatenate([t_real, t_imag], axis=0).astype(BF16)

    for part in range(2):
        span = pl.ds(part * half, half)
        await_all(u_buf.at[:, span], local_sem.at[2 + part])
        second_real = contract_last(packed, u_buf[0, span])
        second_imag = contract_last(packed, u_buf[1, span])
        recv1[me_r, :, span] = jnp.concatenate(
            [second_real[:8] - second_imag[8:], second_imag[:8] + second_real[8:]], axis=0
        ).astype(BF16)
    await_all(onset_buf, local_sem.at[1])
    pltpu.make_async_copy(omega_hbm, omega_ref, local_sem.at[1]).wait()
    pl.semaphore_wait(barrier, n_row + n_col - 1 + (1 - freq) * (n_row - 1))

    @pl.when(freq == 0)
    def _():
        for device in hubs_r + [{"tm": 1}]:
            push(recv1.at[me_r], recv1.at[me_r], 0, device)

    @pl.when(freq == 1)
    def _():
        for device in hubs_r:
            push(recv1.at[me_r], recv1.at[me_r], 3, device)

    for side in range(2):
        g = gram(onset_buf[side], omega_ref[0], omega_ref[1])
        for place, entry in enumerate(entries):
            gram_buf[side, place] = g[entry]

    @pl.when(freq == 0)
    def _():
        await_all(back1, rsem.at[0])

    @pl.when(freq == 1)
    def _():
        g = kept_gram(0)
        await_all(recv1.at[pl.ds(0, n_col - 1)], rsem.at[3])
        near = add(recv1, range(1, 2 * n_col, 2))
        near = [g[m, 2] * near[0] + g[m, 3] * near[1] for m in range(4)]
        await_all(recv1.at[pl.ds(0, n_col)], rsem.at[0])
        y = add(recv1, range(0, 2 * n_col, 2))
        for m in range(2):
            hand1[8 * m : 8 * m + 8] = (g[m, 0] * y[0] + g[m, 1] * y[1] + near[m]).astype(BF16)
        push(hand1, back1, 0, {"tm": 0})
        back1[...] = jnp.concatenate(
            [g[m, 0] * y[0] + g[m, 1] * y[1] + near[m] for m in (2, 3)], axis=0
        ).astype(BF16)

    rows_back = back1[...]
    first_real = contract_inner(rows_back, u_buf[0])
    first_imag = contract_inner(rows_back, u_buf[1])
    s_real = jnp.where(keep, first_real[:8] + first_imag[8:], 0.0)
    s_imag = jnp.where(keep, first_real[8:] - first_imag[:8], 0.0)
    packed_back = jnp.concatenate([s_real, s_imag], axis=0).astype(BF16)
    second_real = contract_inner(packed_back, v_buf[0])
    second_imag = contract_inner(packed_back, v_buf[1])
    recv2[me_s] = jnp.concatenate(
        [second_real[:8] + second_imag[8:], second_real[8:] - second_imag[:8]], axis=0
    ).astype(BF16)
    own = [2 * place for place in range(n_row)]
    far = [2 * place + 1 for place in range(n_row)]

    @pl.when(freq == 0)
    def _():
        for group in (hubs_s[:1], hubs_s[1:]):
            for tm in (0, 1):
                for device in group:
                    push(recv2.at[me_s], recv2.at[me_s], 1, {**device, "tm": tm})
        push(recv2.at[me_s], recv2.at[me_s], 1, {"tm": 1})
        minus_ref[0, 0] = rows_back[:8]
        minus_ref[0, 1] = rows_back[8:]
        await_all(hand2, rsem.at[2])
        await_all(recv2.at[pl.ds(0, n_row - 1)], rsem.at[1])
        g, y = kept_gram(1), add(recv2, own)
        for m in range(2):
            last = hand2[8 * m : 8 * m + 8].astype(F32)
            plus_ref[0, m] = start_buf[m] - (g[m, 0] * y[0] + g[m, 1] * y[1] + last)

    @pl.when(freq == 1)
    def _():
        for device in hubs_s:
            push(recv2.at[me_s], recv2.at[me_s], 2, device)
        minus_ref[0, 0] = rows_back[:8]
        minus_ref[0, 1] = rows_back[8:]
        await_all(recv2.at[pl.ds(0, n_row - 1)], rsem.at[2])
        g, y = kept_gram(1), add(recv2, far)
        back2[...] = jnp.concatenate(
            [g[m, 2] * y[0] + g[m, 3] * y[1] for m in range(2)], axis=0
        ).astype(BF16)
        push(back2, hand2, 2, {"tm": 0})
        await_all(recv2.at[pl.ds(0, n_row)], rsem.at[1])
        x = add(recv2, own)
        done = apply_gram(g, x + y)
        for m in range(2):
            plus_ref[0, m] = start_buf[m] - done[2 + m]

    await_all(recv1.at[pl.ds(0, n_col)], ssem)
    await_all(recv2.at[pl.ds(0, n_row)], ssem)

    @pl.when(freq == 0)
    def _():
        await_all(recv2.at[pl.ds(0, n_row - 1)], ssem)


def epilogue(plus_ref, minus_ref, plus_out, minus_out, sem):
    copies = [
        pltpu.make_async_copy(plus_ref, plus_out, sem.at[0]),
        pltpu.make_async_copy(minus_ref, minus_out, sem.at[1]),
    ]
    for copy in copies:
        copy.start()
    for copy in copies:
        copy.wait()


def per_device(start_field, u_tiles, v_tiles, rank_blocks, onset_receiver, onset_source, omega):
    n_row = lax.axis_size("trow")
    n_col = lax.axis_size("tcol")
    tile_r, tile_s = u_tiles.shape[2], v_tiles.shape[3]
    hbm = pl.BlockSpec(memory_space=pl.ANY)
    vmem = pl.BlockSpec(memory_space=pltpu.VMEM)
    sems = pltpu.SemaphoreType.DMA
    shapes = (
        jax.ShapeDtypeStruct((1, 2, 8, tile_s), F32),
        jax.ShapeDtypeStruct((1, 2, 8, tile_r), BF16),
    )
    plus, minus = pl.pallas_call(
        functools.partial(kernel, n_row, n_col),
        out_shape=shapes,
        in_specs=[hbm] * 3 + [pl.BlockSpec(memory_space=pltpu.SMEM)] + [hbm] * 3,
        out_specs=(vmem, vmem),
        scratch_shapes=[
            pltpu.VMEM(start_field.shape[1:], F32),
            pltpu.VMEM(u_tiles.shape[1:], BF16),
            pltpu.VMEM(v_tiles.shape[1:], BF16),
            pltpu.SMEM((2,), F32),
            pltpu.VMEM((2, 8, tile_r), jnp.int32),
            pltpu.VMEM((2, 10, 8, tile_r), F32),
            pltpu.VMEM((2 * n_col, 16, tile_r), BF16),
            pltpu.VMEM((16, tile_r), BF16),
            pltpu.VMEM((16, tile_r), BF16),
            pltpu.VMEM((2 * n_row, 16, tile_s), BF16),
            pltpu.VMEM((16, tile_s), BF16),
            pltpu.VMEM((16, tile_s), BF16),
            sems((5,)),
            sems(()),
            sems((4,)),
        ],
        compiler_params=pltpu.CompilerParams(
            collective_id=0, has_side_effects=True, vmem_limit_bytes=24 * 1024 * 1024
        ),
    )(
        pin(start_field), pin(u_tiles), pin(v_tiles), rank_blocks,
        pin(onset_receiver), pin(onset_source), pin(omega),
    )
    return pl.pallas_call(
        epilogue,
        out_shape=shapes,
        in_specs=[vmem, vmem],
        out_specs=(pl.BlockSpec(memory_space=pltpu.HBM),) * 2,
        scratch_shapes=[sems((2,))],
    )(
        pltpu.with_memory_space_constraint(plus, pltpu.VMEM),
        pltpu.with_memory_space_constraint(minus, pltpu.VMEM),
    )


def pin(x):
    return pltpu.with_memory_space_constraint(x, pltpu.MemorySpace.HBM)


def solution(mesh):
    placed = (
        P("tm", None, None, "tcol"),
        P("tm", None, "trow", "tcol"),
        P("tm", None, "trow", "tcol"),
        P("tm", "trow", "tcol"),
        P(None, "trow"),
        P(None, "tcol"),
        P(),
    )
    return jax.shard_map(
        per_device,
        mesh=mesh,
        in_specs=placed,
        out_specs=(P("tm", None, None, "tcol"), P("tm", None, None, "trow")),
        check_vma=False,
    )
```

```python
import functools

import jax
import jax.numpy as jnp
from jax import lax
from jax.experimental import pallas as pl
from jax.experimental.pallas import tpu as pltpu
from jax.sharding import PartitionSpec as P

RBLK = 256
NT = 1024
MESH = pl.DeviceIdType.MESH
F32 = jnp.float32
BF16 = jnp.bfloat16


def contract_last(left_side, right_side):
    return lax.dot_general(
        left_side, right_side, (((1,), (1,)), ((), ())), preferred_element_type=F32
    )


def contract_inner(left_side, right_side):
    return lax.dot_general(
        left_side, right_side, (((1,), (0,)), ((), ())), preferred_element_type=F32
    )


def sin_cos(angle):
    turns = jnp.floor(angle * 0.6366197723675814 + 0.5)
    rest = angle - turns * 1.5703125
    rest = rest - turns * 4.837512969970703e-4
    rest = rest - turns * 7.549789948768648e-8
    square = rest * rest
    sine = rest + rest * square * (
        -1.6666654611e-1 + square * (8.3321608736e-3 - square * 1.9515295891e-4)
    )
    cosine = 1.0 - 0.5 * square + square * square * (
        4.166664568298827e-2 + square * (-1.388731625493765e-3 + square * 2.443315711809948e-5)
    )
    quarter = turns - 4.0 * jnp.floor(turns * 0.25)
    swap = (quarter == 1.0) | (quarter == 3.0)
    first = jnp.where(swap, cosine, sine)
    second = jnp.where(swap, sine, cosine)
    first = jnp.where(quarter >= 2.0, -first, first)
    second = jnp.where((quarter == 1.0) | (quarter == 2.0), -second, second)
    return first, second


def prefix_sums(phi, count):
    sine, cosine = sin_cos(phi)
    sine_n, cosine_n = sin_cos(count * phi)
    still = phi == 0.0
    ratio = jnp.where(still, count, sine_n / jnp.where(still, 1.0, sine))
    cos_sum = ratio * (cosine_n * cosine + sine_n * sine)
    sin_sum = ratio * (sine_n * cosine - cosine_n * sine)
    return cos_sum, sin_sum


def gram(onset, omega_a, omega_b):
    count = onset.astype(F32)
    omega_a = jnp.full(count.shape, omega_a, F32)
    omega_b = jnp.full(count.shape, omega_b, F32)
    cos_aa, sin_aa = prefix_sums(omega_a, count)
    cos_bb, sin_bb = prefix_sums(omega_b, count)
    cos_sum, sin_sum = prefix_sums(0.5 * (omega_a + omega_b), count)
    cos_dif, sin_dif = prefix_sums(0.5 * (omega_a - omega_b), count)
    scale = 1.0 / NT
    g = {}
    g[0, 0] = scale * (count + cos_aa)
    g[1, 1] = scale * (count - cos_aa)
    g[0, 1] = -scale * sin_aa
    g[2, 2] = scale * (count + cos_bb)
    g[3, 3] = scale * (count - cos_bb)
    g[2, 3] = -scale * sin_bb
    g[0, 2] = scale * (cos_dif + cos_sum)
    g[1, 3] = scale * (cos_dif - cos_sum)
    g[0, 3] = -scale * (sin_sum - sin_dif)
    g[1, 2] = -scale * (sin_sum + sin_dif)
    for m in range(4):
        for n in range(m):
            g[m, n] = g[n, m]
    return g


def apply_gram(g, y):
    return [
        g[m, 0] * y[0] + g[m, 1] * y[1] + g[m, 2] * y[2] + g[m, 3] * y[3] for m in range(4)
    ]


def from_zero(me, count):
    return [step + (step + count - me) // count for step in range(count - 1)]


def kernel(
    n_row, n_col,
    start_hbm, u_hbm, v_hbm, rank_ref, onset_r_hbm, onset_s_hbm, omega_hbm,
    plus_ref, minus_ref,
    start_buf, u_buf, v_buf, omega_ref, onset_buf, gram_buf,
    recv1, hand1, back1, recv2, hand2, back2,
    local_sem, ssem, rsem,
):
    row = lax.axis_index("trow")
    col = lax.axis_index("tcol")
    freq = lax.axis_index("tm")
    me_r, me_s = col * 2 + freq, row * 2 + freq
    half = u_buf.shape[1] // 2

    for place, source, target in (
        (0, start_hbm.at[0], start_buf),
        (0, v_hbm.at[0, 0], v_buf.at[0]),
        (4, v_hbm.at[0, 1], v_buf.at[1]),
        (1, omega_hbm, omega_ref),
        (2, u_hbm.at[0, :, pl.ds(0, half)], u_buf.at[:, pl.ds(0, half)]),
        (3, u_hbm.at[0, :, pl.ds(half, half)], u_buf.at[:, pl.ds(half, half)]),
        (1, onset_r_hbm, onset_buf.at[0]),
        (1, onset_s_hbm, onset_buf.at[1]),
    ):
        pltpu.make_async_copy(source, target, local_sem.at[place]).start()

    def await_all(ref, sem):
        pltpu.make_async_copy(ref, ref, sem).wait()

    hubs_r = [{"tcol": place, "tm": 1} for place in from_zero(col, n_col)]
    hubs_s = [{"trow": place, "tm": 1} for place in from_zero(row, n_row)]
    barrier = pltpu.get_barrier_semaphore()

    def signal(device):
        pl.semaphore_signal(barrier, inc=1, device_id=device, device_id_type=MESH)

    @pl.when(freq == 1)
    def _():
        for device in hubs_r + hubs_s:
            signal(device)
            signal({**device, "tm": 0})

    @pl.when(freq == 0)
    def _():
        for device in hubs_s:
            signal({**device, "tm": 0})

    signal({"tm": 1 - freq})

    def push(source, target, sem, device):
        pltpu.make_async_remote_copy(
            src_ref=source, dst_ref=target, send_sem=ssem, recv_sem=rsem.at[sem],
            device_id=device, device_id_type=MESH,
        ).start()

    def add(recv, places):
        total = recv[places[0]].astype(F32)
        for place in places[1:]:
            total = total + recv[place].astype(F32)
        return [total[:8], total[8:]]

    entries = [(m, n) for m in range(4) for n in range(m, 4)]

    def kept_gram(side):
        g = {}
        for place, (m, n) in enumerate(entries):
            g[m, n] = g[n, m] = gram_buf[side, place]
        return g

    await_all(start_buf, local_sem.at[0])
    await_all(v_buf.at[0], local_sem.at[0])
    rows_in = jnp.concatenate([start_buf[0], start_buf[1]], axis=0).astype(BF16)
    first_real = contract_last(rows_in, v_buf[0])
    await_all(v_buf.at[1], local_sem.at[4])
    first_imag = contract_last(rows_in, v_buf[1])
    lane = lax.broadcasted_iota(jnp.int32, (8, first_real.shape[1]), 1)
    keep = lane < rank_ref[0, 0, 0] * RBLK
    t_real = jnp.where(keep, first_real[:8] - first_imag[8:], 0.0)
    t_imag = jnp.where(keep, first_imag[:8] + first_real[8:], 0.0)
    packed = jnp.concatenate([t_real, t_imag], axis=0).astype(BF16)

    for part in range(2):
        span = pl.ds(part * half, half)
        await_all(u_buf.at[:, span], local_sem.at[2 + part])
        second_real = contract_last(packed, u_buf[0, span])
        second_imag = contract_last(packed, u_buf[1, span])
        recv1[me_r, :, span] = jnp.concatenate(
            [second_real[:8] - second_imag[8:], second_imag[:8] + second_real[8:]], axis=0
        ).astype(BF16)
        if part == 0:
            pl.semaphore_wait(barrier, n_row + n_col - 1 + (1 - freq) * (n_row - 1))
        push(recv1.at[me_r, :, span], recv1.at[me_r, :, span], 3 * freq, hubs_r[0])
    await_all(onset_buf, local_sem.at[1])
    pltpu.make_async_copy(omega_hbm, omega_ref, local_sem.at[1]).wait()
    for device in hubs_r[1:]:
        push(recv1.at[me_r], recv1.at[me_r], 3 * freq, device)

    @pl.when(freq == 0)
    def _():
        push(recv1.at[me_r], recv1.at[me_r], 0, {"tm": 1})

    for side in range(2):
        g = gram(onset_buf[side], omega_ref[0], omega_ref[1])
        for place, entry in enumerate(entries):
            gram_buf[side, place] = g[entry]

    @pl.when(freq == 0)
    def _():
        await_all(back1, rsem.at[0])

    @pl.when(freq == 1)
    def _():
        g = kept_gram(0)
        await_all(recv1.at[pl.ds(0, n_col - 1)], rsem.at[3])
        near = add(recv1, range(1, 2 * n_col, 2))
        near = [g[m, 2] * near[0] + g[m, 3] * near[1] for m in range(4)]
        await_all(recv1.at[pl.ds(0, n_col)], rsem.at[0])
        y = add(recv1, range(0, 2 * n_col, 2))
        for m in range(2):
            hand1[8 * m : 8 * m + 8] = (g[m, 0] * y[0] + g[m, 1] * y[1] + near[m]).astype(BF16)
        push(hand1, back1, 0, {"tm": 0})
        back1[...] = jnp.concatenate(
            [g[m, 0] * y[0] + g[m, 1] * y[1] + near[m] for m in (2, 3)], axis=0
        ).astype(BF16)

    rows_back = back1[...]
    first_real = contract_inner(rows_back, u_buf[0])
    first_imag = contract_inner(rows_back, u_buf[1])
    s_real = jnp.where(keep, first_real[:8] + first_imag[8:], 0.0)
    s_imag = jnp.where(keep, first_real[8:] - first_imag[:8], 0.0)
    packed_back = jnp.concatenate([s_real, s_imag], axis=0).astype(BF16)
    half_s = v_buf.shape[2] // 2
    for part in range(2):
        span = pl.ds(part * half_s, half_s)
        second_real = contract_inner(packed_back, v_buf[0, :, span])
        second_imag = contract_inner(packed_back, v_buf[1, :, span])
        recv2[me_s, :, span] = jnp.concatenate(
            [second_real[:8] + second_imag[8:], second_real[8:] - second_imag[:8]], axis=0
        ).astype(BF16)

        @pl.when(freq == 0)
        def _():
            push(recv2.at[me_s, :, span], recv2.at[me_s, :, span], 1, {**hubs_s[0], "tm": 0})
    own = [2 * place for place in range(n_row)]
    far = [2 * place + 1 for place in range(n_row)]

    @pl.when(freq == 0)
    def _():
        push(recv2.at[me_s], recv2.at[me_s], 1, hubs_s[0])
        for tm in (0, 1):
            for device in hubs_s[1:]:
                push(recv2.at[me_s], recv2.at[me_s], 1, {**device, "tm": tm})
        push(recv2.at[me_s], recv2.at[me_s], 1, {"tm": 1})
        minus_ref[0, 0] = rows_back[:8]
        minus_ref[0, 1] = rows_back[8:]
        await_all(hand2, rsem.at[2])
        await_all(recv2.at[pl.ds(0, n_row - 1)], rsem.at[1])
        g, y = kept_gram(1), add(recv2, own)
        for m in range(2):
            last = hand2[8 * m : 8 * m + 8].astype(F32)
            plus_ref[0, m] = start_buf[m] - (g[m, 0] * y[0] + g[m, 1] * y[1] + last)

    @pl.when(freq == 1)
    def _():
        for device in hubs_s:
            push(recv2.at[me_s], recv2.at[me_s], 2, device)
        minus_ref[0, 0] = rows_back[:8]
        minus_ref[0, 1] = rows_back[8:]
        await_all(recv2.at[pl.ds(0, n_row - 1)], rsem.at[2])
        g, y = kept_gram(1), add(recv2, far)
        back2[...] = jnp.concatenate(
            [g[m, 2] * y[0] + g[m, 3] * y[1] for m in range(2)], axis=0
        ).astype(BF16)
        push(back2, hand2, 2, {"tm": 0})
        await_all(recv2.at[pl.ds(0, n_row)], rsem.at[1])
        x = add(recv2, own)
        done = apply_gram(g, x + y)
        for m in range(2):
            plus_ref[0, m] = start_buf[m] - done[2 + m]

    await_all(recv1.at[pl.ds(0, n_col)], ssem)
    await_all(recv2.at[pl.ds(0, n_row)], ssem)

    @pl.when(freq == 0)
    def _():
        await_all(recv2.at[pl.ds(0, n_row - 1)], ssem)


def epilogue(plus_ref, minus_ref, plus_out, minus_out, sem):
    copies = [
        pltpu.make_async_copy(plus_ref, plus_out, sem.at[0]),
        pltpu.make_async_copy(minus_ref, minus_out, sem.at[1]),
    ]
    for copy in copies:
        copy.start()
    for copy in copies:
        copy.wait()


def per_device(start_field, u_tiles, v_tiles, rank_blocks, onset_receiver, onset_source, omega):
    n_row = lax.axis_size("trow")
    n_col = lax.axis_size("tcol")
    tile_r, tile_s = u_tiles.shape[2], v_tiles.shape[3]
    hbm = pl.BlockSpec(memory_space=pl.ANY)
    vmem = pl.BlockSpec(memory_space=pltpu.VMEM)
    sems = pltpu.SemaphoreType.DMA
    shapes = (
        jax.ShapeDtypeStruct((1, 2, 8, tile_s), F32),
        jax.ShapeDtypeStruct((1, 2, 8, tile_r), BF16),
    )
    plus, minus = pl.pallas_call(
        functools.partial(kernel, n_row, n_col),
        out_shape=shapes,
        in_specs=[hbm] * 3 + [pl.BlockSpec(memory_space=pltpu.SMEM)] + [hbm] * 3,
        out_specs=(vmem, vmem),
        scratch_shapes=[
            pltpu.VMEM(start_field.shape[1:], F32),
            pltpu.VMEM(u_tiles.shape[1:], BF16),
            pltpu.VMEM(v_tiles.shape[1:], BF16),
            pltpu.SMEM((2,), F32),
            pltpu.VMEM((2, 8, tile_r), jnp.int32),
            pltpu.VMEM((2, 10, 8, tile_r), F32),
            pltpu.VMEM((2 * n_col, 16, tile_r), BF16),
            pltpu.VMEM((16, tile_r), BF16),
            pltpu.VMEM((16, tile_r), BF16),
            pltpu.VMEM((2 * n_row, 16, tile_s), BF16),
            pltpu.VMEM((16, tile_s), BF16),
            pltpu.VMEM((16, tile_s), BF16),
            sems((5,)),
            sems(()),
            sems((4,)),
        ],
        compiler_params=pltpu.CompilerParams(
            collective_id=0, has_side_effects=True, vmem_limit_bytes=24 * 1024 * 1024
        ),
    )(
        pin(start_field), pin(u_tiles), pin(v_tiles), rank_blocks,
        pin(onset_receiver), pin(onset_source), pin(omega),
    )
    return pl.pallas_call(
        epilogue,
        out_shape=shapes,
        in_specs=[vmem, vmem],
        out_specs=(pl.BlockSpec(memory_space=pltpu.HBM),) * 2,
        scratch_shapes=[sems((2,))],
    )(
        pltpu.with_memory_space_constraint(plus, pltpu.VMEM),
        pltpu.with_memory_space_constraint(minus, pltpu.VMEM),
    )


def pin(x):
    return pltpu.with_memory_space_constraint(x, pltpu.MemorySpace.HBM)


def solution(mesh):
    placed = (
        P("tm", None, None, "tcol"),
        P("tm", None, "trow", "tcol"),
        P("tm", None, "trow", "tcol"),
        P("tm", "trow", "tcol"),
        P(None, "trow"),
        P(None, "tcol"),
        P(),
    )
    return jax.shard_map(
        per_device,
        mesh=mesh,
        in_specs=placed,
        out_specs=(P("tm", None, None, "tcol"), P("tm", None, None, "trow")),
        check_vma=False,
    )
```

```python
import functools

import jax
import jax.numpy as jnp
from jax import lax
from jax.experimental import pallas as pl
from jax.experimental.pallas import tpu as pltpu
from jax.sharding import PartitionSpec as P

RBLK = 256
NT = 1024
MESH = pl.DeviceIdType.MESH
F32 = jnp.float32
BF16 = jnp.bfloat16


def contract_last(left_side, right_side):
    return lax.dot_general(
        left_side, right_side, (((1,), (1,)), ((), ())), preferred_element_type=F32
    )


def contract_inner(left_side, right_side):
    return lax.dot_general(
        left_side, right_side, (((1,), (0,)), ((), ())), preferred_element_type=F32
    )


def sin_cos(angle):
    turns = jnp.floor(angle * 0.6366197723675814 + 0.5)
    rest = angle - turns * 1.5703125
    rest = rest - turns * 4.837512969970703e-4
    rest = rest - turns * 7.549789948768648e-8
    square = rest * rest
    sine = rest + rest * square * (
        -1.6666654611e-1 + square * (8.3321608736e-3 - square * 1.9515295891e-4)
    )
    cosine = 1.0 - 0.5 * square + square * square * (
        4.166664568298827e-2 + square * (-1.388731625493765e-3 + square * 2.443315711809948e-5)
    )
    quarter = turns - 4.0 * jnp.floor(turns * 0.25)
    swap = (quarter == 1.0) | (quarter == 3.0)
    first = jnp.where(swap, cosine, sine)
    second = jnp.where(swap, sine, cosine)
    first = jnp.where(quarter >= 2.0, -first, first)
    second = jnp.where((quarter == 1.0) | (quarter == 2.0), -second, second)
    return first, second


def prefix_sums(phi, count):
    sine, cosine = sin_cos(phi)
    sine_n, cosine_n = sin_cos(count * phi)
    still = phi == 0.0
    ratio = jnp.where(still, count, sine_n / jnp.where(still, 1.0, sine))
    cos_sum = ratio * (cosine_n * cosine + sine_n * sine)
    sin_sum = ratio * (sine_n * cosine - cosine_n * sine)
    return cos_sum, sin_sum


def gram(onset, omega_a, omega_b):
    count = onset.astype(F32)
    omega_a = jnp.full(count.shape, omega_a, F32)
    omega_b = jnp.full(count.shape, omega_b, F32)
    cos_aa, sin_aa = prefix_sums(omega_a, count)
    cos_bb, sin_bb = prefix_sums(omega_b, count)
    cos_sum, sin_sum = prefix_sums(0.5 * (omega_a + omega_b), count)
    cos_dif, sin_dif = prefix_sums(0.5 * (omega_a - omega_b), count)
    scale = 1.0 / NT
    g = {}
    g[0, 0] = scale * (count + cos_aa)
    g[1, 1] = scale * (count - cos_aa)
    g[0, 1] = -scale * sin_aa
    g[2, 2] = scale * (count + cos_bb)
    g[3, 3] = scale * (count - cos_bb)
    g[2, 3] = -scale * sin_bb
    g[0, 2] = scale * (cos_dif + cos_sum)
    g[1, 3] = scale * (cos_dif - cos_sum)
    g[0, 3] = -scale * (sin_sum - sin_dif)
    g[1, 2] = -scale * (sin_sum + sin_dif)
    for m in range(4):
        for n in range(m):
            g[m, n] = g[n, m]
    return g


def apply_gram(g, y):
    return [
        g[m, 0] * y[0] + g[m, 1] * y[1] + g[m, 2] * y[2] + g[m, 3] * y[3] for m in range(4)
    ]


def from_zero(me, count):
    return [step + (step + count - me) // count for step in range(count - 1)]


def kernel(
    n_row, n_col,
    start_hbm, u_hbm, v_hbm, rank_ref, onset_r_hbm, onset_s_hbm, omega_hbm,
    plus_ref, minus_ref,
    start_buf, u_buf, v_buf, omega_ref, onset_buf, gram_buf,
    recv1, hand1, back1, recv2, hand2, back2,
    local_sem, ssem, rsem,
):
    row = lax.axis_index("trow")
    col = lax.axis_index("tcol")
    freq = lax.axis_index("tm")
    me_r, me_s = col * 2 + freq, row * 2 + freq
    half = u_buf.shape[1] // 2

    for place, source, target in (
        (0, start_hbm.at[0], start_buf),
        (0, v_hbm.at[0, 0], v_buf.at[0]),
        (4, v_hbm.at[0, 1], v_buf.at[1]),
        (1, omega_hbm, omega_ref),
        (2, u_hbm.at[0, :, pl.ds(0, half)], u_buf.at[:, pl.ds(0, half)]),
        (3, u_hbm.at[0, :, pl.ds(half, half)], u_buf.at[:, pl.ds(half, half)]),
        (1, onset_r_hbm, onset_buf.at[0]),
        (1, onset_s_hbm, onset_buf.at[1]),
    ):
        pltpu.make_async_copy(source, target, local_sem.at[place]).start()

    def await_all(ref, sem):
        pltpu.make_async_copy(ref, ref, sem).wait()

    hubs_r = [{"tcol": place, "tm": 1} for place in from_zero(col, n_col)]
    hubs_s = [{"trow": place, "tm": 1} for place in from_zero(row, n_row)]
    barrier = pltpu.get_barrier_semaphore()

    def signal(device):
        pl.semaphore_signal(barrier, inc=1, device_id=device, device_id_type=MESH)

    @pl.when(freq == 1)
    def _():
        for device in hubs_r + hubs_s:
            signal(device)
            signal({**device, "tm": 0})

    @pl.when(freq == 0)
    def _():
        for device in hubs_s:
            signal({**device, "tm": 0})

    signal({"tm": 1 - freq})

    def push(source, target, sem, device):
        pltpu.make_async_remote_copy(
            src_ref=source, dst_ref=target, send_sem=ssem, recv_sem=rsem.at[sem],
            device_id=device, device_id_type=MESH,
        ).start()

    def add(recv, places):
        total = recv[places[0]].astype(F32)
        for place in places[1:]:
            total = total + recv[place].astype(F32)
        return [total[:8], total[8:]]

    entries = [(m, n) for m in range(4) for n in range(m, 4)]

    def kept_gram(side):
        g = {}
        for place, (m, n) in enumerate(entries):
            g[m, n] = g[n, m] = gram_buf[side, place]
        return g

    await_all(start_buf, local_sem.at[0])
    await_all(v_buf.at[0], local_sem.at[0])
    rows_in = jnp.concatenate([start_buf[0], start_buf[1]], axis=0).astype(BF16)
    first_real = contract_last(rows_in, v_buf[0])
    await_all(v_buf.at[1], local_sem.at[4])
    first_imag = contract_last(rows_in, v_buf[1])
    lane = lax.broadcasted_iota(jnp.int32, (8, first_real.shape[1]), 1)
    keep = lane < rank_ref[0, 0, 0] * RBLK
    t_real = jnp.where(keep, first_real[:8] - first_imag[8:], 0.0)
    t_imag = jnp.where(keep, first_imag[:8] + first_real[8:], 0.0)
    packed = jnp.concatenate([t_real, t_imag], axis=0).astype(BF16)

    for part in range(2):
        span = pl.ds(part * half, half)
        await_all(u_buf.at[:, span], local_sem.at[2 + part])
        second_real = contract_last(packed, u_buf[0, span])
        second_imag = contract_last(packed, u_buf[1, span])
        recv1[me_r, :, span] = jnp.concatenate(
            [second_real[:8] - second_imag[8:], second_imag[:8] + second_real[8:]], axis=0
        ).astype(BF16)
        if part == 0:
            pl.semaphore_wait(barrier, n_row + n_col - 1 + (1 - freq) * (n_row - 1))
        push(recv1.at[me_r, :, span], recv1.at[me_r, :, span], 3 * freq, hubs_r[0])
    await_all(onset_buf, local_sem.at[1])
    pltpu.make_async_copy(omega_hbm, omega_ref, local_sem.at[1]).wait()

    @pl.when(freq == 0)
    def _():
        push(recv1.at[me_r], recv1.at[me_r], 0, {"tm": 1})

    for side in (0,):
        g = gram(onset_buf[side], omega_ref[0], omega_ref[1])
        for place, entry in enumerate(entries):
            gram_buf[side, place] = g[entry]

    for device in hubs_r[1:]:
        push(recv1.at[me_r], recv1.at[me_r], 3 * freq, device)

    for side in (1,):
        g = gram(onset_buf[side], omega_ref[0], omega_ref[1])
        for place, entry in enumerate(entries):
            gram_buf[side, place] = g[entry]

    @pl.when(freq == 0)
    def _():
        await_all(back1, rsem.at[0])

    @pl.when(freq == 1)
    def _():
        g = kept_gram(0)
        await_all(recv1.at[pl.ds(0, n_col - 1)], rsem.at[3])
        near = add(recv1, range(1, 2 * n_col, 2))
        near = [g[m, 2] * near[0] + g[m, 3] * near[1] for m in range(4)]
        await_all(recv1.at[pl.ds(0, n_col)], rsem.at[0])
        y = add(recv1, range(0, 2 * n_col, 2))
        for m in range(2):
            hand1[8 * m : 8 * m + 8] = (g[m, 0] * y[0] + g[m, 1] * y[1] + near[m]).astype(BF16)
        push(hand1, back1, 0, {"tm": 0})
        back1[...] = jnp.concatenate(
            [g[m, 0] * y[0] + g[m, 1] * y[1] + near[m] for m in (2, 3)], axis=0
        ).astype(BF16)

    rows_back = back1[...]
    first_real = contract_inner(rows_back, u_buf[0])
    first_imag = contract_inner(rows_back, u_buf[1])
    s_real = jnp.where(keep, first_real[:8] + first_imag[8:], 0.0)
    s_imag = jnp.where(keep, first_real[8:] - first_imag[:8], 0.0)
    packed_back = jnp.concatenate([s_real, s_imag], axis=0).astype(BF16)
    half_s = v_buf.shape[2] // 2
    for part in range(2):
        span = pl.ds(part * half_s, half_s)
        second_real = contract_inner(packed_back, v_buf[0, :, span])
        second_imag = contract_inner(packed_back, v_buf[1, :, span])
        recv2[me_s, :, span] = jnp.concatenate(
            [second_real[:8] + second_imag[8:], second_real[8:] - second_imag[:8]], axis=0
        ).astype(BF16)

        @pl.when(freq == 0)
        def _():
            push(recv2.at[me_s, :, span], recv2.at[me_s, :, span], 1, {**hubs_s[0], "tm": 0})
    own = [2 * place for place in range(n_row)]
    far = [2 * place + 1 for place in range(n_row)]

    @pl.when(freq == 0)
    def _():
        push(recv2.at[me_s], recv2.at[me_s], 1, hubs_s[0])
        for tm in (0, 1):
            for device in hubs_s[1:]:
                push(recv2.at[me_s], recv2.at[me_s], 1, {**device, "tm": tm})
        push(recv2.at[me_s], recv2.at[me_s], 1, {"tm": 1})
        minus_ref[0, 0] = rows_back[:8]
        minus_ref[0, 1] = rows_back[8:]
        await_all(hand2, rsem.at[2])
        await_all(recv2.at[pl.ds(0, n_row - 1)], rsem.at[1])
        g, y = kept_gram(1), add(recv2, own)
        for m in range(2):
            last = hand2[8 * m : 8 * m + 8].astype(F32)
            plus_ref[0, m] = start_buf[m] - (g[m, 0] * y[0] + g[m, 1] * y[1] + last)

    @pl.when(freq == 1)
    def _():
        for device in hubs_s:
            push(recv2.at[me_s], recv2.at[me_s], 2, device)
        minus_ref[0, 0] = rows_back[:8]
        minus_ref[0, 1] = rows_back[8:]
        await_all(recv2.at[pl.ds(0, n_row - 1)], rsem.at[2])
        g, y = kept_gram(1), add(recv2, far)
        back2[...] = jnp.concatenate(
            [g[m, 2] * y[0] + g[m, 3] * y[1] for m in range(2)], axis=0
        ).astype(BF16)
        push(back2, hand2, 2, {"tm": 0})
        await_all(recv2.at[pl.ds(0, n_row)], rsem.at[1])
        x = add(recv2, own)
        done = apply_gram(g, x + y)
        for m in range(2):
            plus_ref[0, m] = start_buf[m] - done[2 + m]

    await_all(recv1.at[pl.ds(0, n_col)], ssem)
    await_all(recv2.at[pl.ds(0, n_row)], ssem)

    @pl.when(freq == 0)
    def _():
        await_all(recv2.at[pl.ds(0, n_row - 1)], ssem)


def epilogue(plus_ref, minus_ref, plus_out, minus_out, sem):
    copies = [
        pltpu.make_async_copy(plus_ref, plus_out, sem.at[0]),
        pltpu.make_async_copy(minus_ref, minus_out, sem.at[1]),
    ]
    for copy in copies:
        copy.start()
    for copy in copies:
        copy.wait()


def per_device(start_field, u_tiles, v_tiles, rank_blocks, onset_receiver, onset_source, omega):
    n_row = lax.axis_size("trow")
    n_col = lax.axis_size("tcol")
    tile_r, tile_s = u_tiles.shape[2], v_tiles.shape[3]
    hbm = pl.BlockSpec(memory_space=pl.ANY)
    vmem = pl.BlockSpec(memory_space=pltpu.VMEM)
    sems = pltpu.SemaphoreType.DMA
    shapes = (
        jax.ShapeDtypeStruct((1, 2, 8, tile_s), F32),
        jax.ShapeDtypeStruct((1, 2, 8, tile_r), BF16),
    )
    plus, minus = pl.pallas_call(
        functools.partial(kernel, n_row, n_col),
        out_shape=shapes,
        in_specs=[hbm] * 3 + [pl.BlockSpec(memory_space=pltpu.SMEM)] + [hbm] * 3,
        out_specs=(vmem, vmem),
        scratch_shapes=[
            pltpu.VMEM(start_field.shape[1:], F32),
            pltpu.VMEM(u_tiles.shape[1:], BF16),
            pltpu.VMEM(v_tiles.shape[1:], BF16),
            pltpu.SMEM((2,), F32),
            pltpu.VMEM((2, 8, tile_r), jnp.int32),
            pltpu.VMEM((2, 10, 8, tile_r), F32),
            pltpu.VMEM((2 * n_col, 16, tile_r), BF16),
            pltpu.VMEM((16, tile_r), BF16),
            pltpu.VMEM((16, tile_r), BF16),
            pltpu.VMEM((2 * n_row, 16, tile_s), BF16),
            pltpu.VMEM((16, tile_s), BF16),
            pltpu.VMEM((16, tile_s), BF16),
            sems((5,)),
            sems(()),
            sems((4,)),
        ],
        compiler_params=pltpu.CompilerParams(
            collective_id=0, has_side_effects=True, vmem_limit_bytes=24 * 1024 * 1024
        ),
    )(
        pin(start_field), pin(u_tiles), pin(v_tiles), rank_blocks,
        pin(onset_receiver), pin(onset_source), pin(omega),
    )
    return pl.pallas_call(
        epilogue,
        out_shape=shapes,
        in_specs=[vmem, vmem],
        out_specs=(pl.BlockSpec(memory_space=pltpu.HBM),) * 2,
        scratch_shapes=[sems((2,))],
    )(
        pltpu.with_memory_space_constraint(plus, pltpu.VMEM),
        pltpu.with_memory_space_constraint(minus, pltpu.VMEM),
    )


def pin(x):
    return pltpu.with_memory_space_constraint(x, pltpu.MemorySpace.HBM)


def solution(mesh):
    placed = (
        P("tm", None, None, "tcol"),
        P("tm", None, "trow", "tcol"),
        P("tm", None, "trow", "tcol"),
        P("tm", "trow", "tcol"),
        P(None, "trow"),
        P(None, "tcol"),
        P(),
    )
    return jax.shard_map(
        per_device,
        mesh=mesh,
        in_specs=placed,
        out_specs=(P("tm", None, None, "tcol"), P("tm", None, None, "trow")),
        check_vma=False,
    )
```

```python
import functools

import jax
import jax.numpy as jnp
from jax import lax
from jax.experimental import pallas as pl
from jax.experimental.pallas import tpu as pltpu
from jax.sharding import PartitionSpec as P

RBLK = 256
NT = 1024
MESH = pl.DeviceIdType.MESH
F32 = jnp.float32
BF16 = jnp.bfloat16


def contract_last(left_side, right_side):
    return lax.dot_general(
        left_side, right_side, (((1,), (1,)), ((), ())), preferred_element_type=F32
    )


def contract_inner(left_side, right_side):
    return lax.dot_general(
        left_side, right_side, (((1,), (0,)), ((), ())), preferred_element_type=F32
    )


def sin_cos(angle):
    turns = jnp.floor(angle * 0.6366197723675814 + 0.5)
    rest = angle - turns * 1.5703125
    rest = rest - turns * 4.837512969970703e-4
    rest = rest - turns * 7.549789948768648e-8
    square = rest * rest
    sine = rest + rest * square * (
        -1.6666654611e-1 + square * (8.3321608736e-3 - square * 1.9515295891e-4)
    )
    cosine = 1.0 - 0.5 * square + square * square * (
        4.166664568298827e-2 + square * (-1.388731625493765e-3 + square * 2.443315711809948e-5)
    )
    quarter = turns - 4.0 * jnp.floor(turns * 0.25)
    swap = (quarter == 1.0) | (quarter == 3.0)
    first = jnp.where(swap, cosine, sine)
    second = jnp.where(swap, sine, cosine)
    first = jnp.where(quarter >= 2.0, -first, first)
    second = jnp.where((quarter == 1.0) | (quarter == 2.0), -second, second)
    return first, second


def prefix_sums(phi, count):
    sine, cosine = sin_cos(phi)
    sine_n, cosine_n = sin_cos(count * phi)
    still = phi == 0.0
    ratio = jnp.where(still, count, sine_n / jnp.where(still, 1.0, sine))
    cos_sum = ratio * (cosine_n * cosine + sine_n * sine)
    sin_sum = ratio * (sine_n * cosine - cosine_n * sine)
    return cos_sum, sin_sum


def gram(onset, omega_a, omega_b):
    count = onset.astype(F32)
    omega_a = jnp.full(count.shape, omega_a, F32)
    omega_b = jnp.full(count.shape, omega_b, F32)
    cos_aa, sin_aa = prefix_sums(omega_a, count)
    cos_bb, sin_bb = prefix_sums(omega_b, count)
    cos_sum, sin_sum = prefix_sums(0.5 * (omega_a + omega_b), count)
    cos_dif, sin_dif = prefix_sums(0.5 * (omega_a - omega_b), count)
    scale = 1.0 / NT
    g = {}
    g[0, 0] = scale * (count + cos_aa)
    g[1, 1] = scale * (count - cos_aa)
    g[0, 1] = -scale * sin_aa
    g[2, 2] = scale * (count + cos_bb)
    g[3, 3] = scale * (count - cos_bb)
    g[2, 3] = -scale * sin_bb
    g[0, 2] = scale * (cos_dif + cos_sum)
    g[1, 3] = scale * (cos_dif - cos_sum)
    g[0, 3] = -scale * (sin_sum - sin_dif)
    g[1, 2] = -scale * (sin_sum + sin_dif)
    for m in range(4):
        for n in range(m):
            g[m, n] = g[n, m]
    return g


def apply_gram(g, y):
    return [
        g[m, 0] * y[0] + g[m, 1] * y[1] + g[m, 2] * y[2] + g[m, 3] * y[3] for m in range(4)
    ]


def from_zero(me, count):
    return [step + (step + count - me) // count for step in range(count - 1)]


def kernel(
    n_row, n_col,
    start_hbm, u_hbm, v_hbm, rank_ref, onset_r_hbm, onset_s_hbm, omega_hbm,
    plus_ref, minus_ref,
    start_buf, u_buf, v_buf, omega_ref, onset_buf, gram_buf,
    recv1, hand1, back1, recv2, hand2, back2,
    local_sem, ssem, rsem,
):
    row = lax.axis_index("trow")
    col = lax.axis_index("tcol")
    freq = lax.axis_index("tm")
    me_r, me_s = col * 2 + freq, row * 2 + freq
    half = u_buf.shape[1] // 2

    for place, source, target in (
        (0, start_hbm.at[0], start_buf),
        (0, v_hbm.at[0, 0], v_buf.at[0]),
        (4, v_hbm.at[0, 1], v_buf.at[1]),
        (1, omega_hbm, omega_ref),
        (2, u_hbm.at[0, :, pl.ds(0, half)], u_buf.at[:, pl.ds(0, half)]),
        (3, u_hbm.at[0, :, pl.ds(half, half)], u_buf.at[:, pl.ds(half, half)]),
        (1, onset_r_hbm, onset_buf.at[0]),
        (1, onset_s_hbm, onset_buf.at[1]),
    ):
        pltpu.make_async_copy(source, target, local_sem.at[place]).start()

    def await_all(ref, sem):
        pltpu.make_async_copy(ref, ref, sem).wait()

    hubs_r = [{"tcol": place, "tm": 1} for place in from_zero(col, n_col)]
    hubs_s = [{"trow": place, "tm": 1} for place in from_zero(row, n_row)]
    barrier = pltpu.get_barrier_semaphore()

    def signal(device):
        pl.semaphore_signal(barrier, inc=1, device_id=device, device_id_type=MESH)

    @pl.when(freq == 1)
    def _():
        for device in hubs_r + hubs_s:
            signal(device)
            signal({**device, "tm": 0})

    @pl.when(freq == 0)
    def _():
        for device in hubs_s:
            signal({**device, "tm": 0})

    signal({"tm": 1 - freq})

    def push(source, target, sem, device):
        pltpu.make_async_remote_copy(
            src_ref=source, dst_ref=target, send_sem=ssem, recv_sem=rsem.at[sem],
            device_id=device, device_id_type=MESH,
        ).start()

    def add(recv, places):
        total = recv[places[0]].astype(F32)
        for place in places[1:]:
            total = total + recv[place].astype(F32)
        return [total[:8], total[8:]]

    entries = [(m, n) for m in range(4) for n in range(m, 4)]

    def kept_gram(side):
        g = {}
        for place, (m, n) in enumerate(entries):
            g[m, n] = g[n, m] = gram_buf[side, place]
        return g

    await_all(start_buf, local_sem.at[0])
    await_all(v_buf.at[0], local_sem.at[0])
    rows_in = jnp.concatenate([start_buf[0], start_buf[1]], axis=0).astype(BF16)
    first_real = contract_last(rows_in, v_buf[0])
    await_all(v_buf.at[1], local_sem.at[4])
    first_imag = contract_last(rows_in, v_buf[1])
    lane = lax.broadcasted_iota(jnp.int32, (8, first_real.shape[1]), 1)
    keep = lane < rank_ref[0, 0, 0] * RBLK
    t_real = jnp.where(keep, first_real[:8] - first_imag[8:], 0.0)
    t_imag = jnp.where(keep, first_imag[:8] + first_real[8:], 0.0)
    packed = jnp.concatenate([t_real, t_imag], axis=0).astype(BF16)

    for part in range(2):
        span = pl.ds(part * half, half)
        await_all(u_buf.at[:, span], local_sem.at[2 + part])
        second_real = contract_last(packed, u_buf[0, span])
        second_imag = contract_last(packed, u_buf[1, span])
        recv1[me_r, :, span] = jnp.concatenate(
            [second_real[:8] - second_imag[8:], second_imag[:8] + second_real[8:]], axis=0
        ).astype(BF16)
        if part == 0:
            pl.semaphore_wait(barrier, n_row + n_col - 1 + (1 - freq) * (n_row - 1))
        push(recv1.at[me_r, :, span], recv1.at[me_r, :, span], 3 * freq, hubs_r[0])
    await_all(onset_buf, local_sem.at[1])
    pltpu.make_async_copy(omega_hbm, omega_ref, local_sem.at[1]).wait()

    @pl.when(freq == 0)
    def _():
        push(recv1.at[me_r], recv1.at[me_r], 0, {"tm": 1})

    for side in (0,):
        g = gram(onset_buf[side], omega_ref[0], omega_ref[1])
        for place, entry in enumerate(entries):
            gram_buf[side, place] = g[entry]

    for device in hubs_r[1:]:
        push(recv1.at[me_r], recv1.at[me_r], 3 * freq, device)

    for side in (1,):
        g = gram(onset_buf[side], omega_ref[0], omega_ref[1])
        for place, entry in enumerate(entries):
            gram_buf[side, place] = g[entry]

    @pl.when(freq == 0)
    def _():
        await_all(back1, rsem.at[0])

    @pl.when(freq == 1)
    def _():
        g = kept_gram(0)
        await_all(recv1.at[pl.ds(0, n_col - 1)], rsem.at[3])
        near = add(recv1, range(1, 2 * n_col, 2))
        near = [g[m, 2] * near[0] + g[m, 3] * near[1] for m in range(4)]
        await_all(recv1.at[pl.ds(0, n_col)], rsem.at[0])
        y = add(recv1, range(0, 2 * n_col, 2))
        hand1[...] = jnp.concatenate(
            [g[m, 0] * y[0] + g[m, 1] * y[1] + near[m] for m in range(2)], axis=0
        ).astype(BF16)
        push(hand1, back1, 0, {"tm": 0})
        back1[...] = jnp.concatenate(
            [g[m, 0] * y[0] + g[m, 1] * y[1] + near[m] for m in (2, 3)], axis=0
        ).astype(BF16)

    rows_back = back1[...]
    first_real = contract_inner(rows_back, u_buf[0])
    first_imag = contract_inner(rows_back, u_buf[1])
    s_real = jnp.where(keep, first_real[:8] + first_imag[8:], 0.0)
    s_imag = jnp.where(keep, first_real[8:] - first_imag[:8], 0.0)
    packed_back = jnp.concatenate([s_real, s_imag], axis=0).astype(BF16)
    half_s = v_buf.shape[2] // 2
    for part in range(2):
        span = pl.ds(part * half_s, half_s)
        second_real = contract_inner(packed_back, v_buf[0, :, span])
        second_imag = contract_inner(packed_back, v_buf[1, :, span])
        recv2[me_s, :, span] = jnp.concatenate(
            [second_real[:8] + second_imag[8:], second_real[8:] - second_imag[:8]], axis=0
        ).astype(BF16)

        @pl.when(freq == 0)
        def _():
            push(recv2.at[me_s, :, span], recv2.at[me_s, :, span], 1, {**hubs_s[0], "tm": 0})
    own = [2 * place for place in range(n_row)]
    far = [2 * place + 1 for place in range(n_row)]

    @pl.when(freq == 0)
    def _():
        push(recv2.at[me_s], recv2.at[me_s], 1, hubs_s[0])
        for tm in (0, 1):
            for device in hubs_s[1:]:
                push(recv2.at[me_s], recv2.at[me_s], 1, {**device, "tm": tm})
        push(recv2.at[me_s], recv2.at[me_s], 1, {"tm": 1})
        minus_ref[0, 0] = rows_back[:8]
        minus_ref[0, 1] = rows_back[8:]
        await_all(hand2, rsem.at[2])
        await_all(recv2.at[pl.ds(0, n_row - 1)], rsem.at[1])
        g, y = kept_gram(1), add(recv2, own)
        last = hand2[...].astype(F32)
        last = [last[:8], last[8:]]
        for m in range(2):
            plus_ref[0, m] = start_buf[m] - (g[m, 0] * y[0] + g[m, 1] * y[1] + last[m])

    @pl.when(freq == 1)
    def _():
        for device in hubs_s:
            push(recv2.at[me_s], recv2.at[me_s], 2, device)
        minus_ref[0, 0] = rows_back[:8]
        minus_ref[0, 1] = rows_back[8:]
        await_all(recv2.at[pl.ds(0, n_row - 1)], rsem.at[2])
        g, y = kept_gram(1), add(recv2, far)
        back2[...] = jnp.concatenate(
            [g[m, 2] * y[0] + g[m, 3] * y[1] for m in range(2)], axis=0
        ).astype(BF16)
        push(back2, hand2, 2, {"tm": 0})
        await_all(recv2.at[pl.ds(0, n_row)], rsem.at[1])
        x = add(recv2, own)
        done = apply_gram(g, x + y)
        for m in range(2):
            plus_ref[0, m] = start_buf[m] - done[2 + m]

    await_all(recv1.at[pl.ds(0, n_col)], ssem)
    await_all(recv2.at[pl.ds(0, n_row)], ssem)

    @pl.when(freq == 0)
    def _():
        await_all(recv2.at[pl.ds(0, n_row - 1)], ssem)


def epilogue(plus_ref, minus_ref, plus_out, minus_out, sem):
    copies = [
        pltpu.make_async_copy(plus_ref, plus_out, sem.at[0]),
        pltpu.make_async_copy(minus_ref, minus_out, sem.at[1]),
    ]
    for copy in copies:
        copy.start()
    for copy in copies:
        copy.wait()


def per_device(start_field, u_tiles, v_tiles, rank_blocks, onset_receiver, onset_source, omega):
    n_row = lax.axis_size("trow")
    n_col = lax.axis_size("tcol")
    tile_r, tile_s = u_tiles.shape[2], v_tiles.shape[3]
    hbm = pl.BlockSpec(memory_space=pl.ANY)
    vmem = pl.BlockSpec(memory_space=pltpu.VMEM)
    sems = pltpu.SemaphoreType.DMA
    shapes = (
        jax.ShapeDtypeStruct((1, 2, 8, tile_s), F32),
        jax.ShapeDtypeStruct((1, 2, 8, tile_r), BF16),
    )
    plus, minus = pl.pallas_call(
        functools.partial(kernel, n_row, n_col),
        out_shape=shapes,
        in_specs=[hbm] * 3 + [pl.BlockSpec(memory_space=pltpu.SMEM)] + [hbm] * 3,
        out_specs=(vmem, vmem),
        scratch_shapes=[
            pltpu.VMEM(start_field.shape[1:], F32),
            pltpu.VMEM(u_tiles.shape[1:], BF16),
            pltpu.VMEM(v_tiles.shape[1:], BF16),
            pltpu.SMEM((2,), F32),
            pltpu.VMEM((2, 8, tile_r), jnp.int32),
            pltpu.VMEM((2, 10, 8, tile_r), F32),
            pltpu.VMEM((2 * n_col, 16, tile_r), BF16),
            pltpu.VMEM((16, tile_r), BF16),
            pltpu.VMEM((16, tile_r), BF16),
            pltpu.VMEM((2 * n_row, 16, tile_s), BF16),
            pltpu.VMEM((16, tile_s), BF16),
            pltpu.VMEM((16, tile_s), BF16),
            sems((5,)),
            sems(()),
            sems((4,)),
        ],
        compiler_params=pltpu.CompilerParams(
            collective_id=0, has_side_effects=True, vmem_limit_bytes=24 * 1024 * 1024
        ),
    )(
        pin(start_field), pin(u_tiles), pin(v_tiles), rank_blocks,
        pin(onset_receiver), pin(onset_source), pin(omega),
    )
    return pl.pallas_call(
        epilogue,
        out_shape=shapes,
        in_specs=[vmem, vmem],
        out_specs=(pl.BlockSpec(memory_space=pltpu.HBM),) * 2,
        scratch_shapes=[sems((2,))],
    )(
        pltpu.with_memory_space_constraint(plus, pltpu.VMEM),
        pltpu.with_memory_space_constraint(minus, pltpu.VMEM),
    )


def pin(x):
    return pltpu.with_memory_space_constraint(x, pltpu.MemorySpace.HBM)


def solution(mesh):
    placed = (
        P("tm", None, None, "tcol"),
        P("tm", None, "trow", "tcol"),
        P("tm", None, "trow", "tcol"),
        P("tm", "trow", "tcol"),
        P(None, "trow"),
        P(None, "tcol"),
        P(),
    )
    return jax.shard_map(
        per_device,
        mesh=mesh,
        in_specs=placed,
        out_specs=(P("tm", None, None, "tcol"), P("tm", None, None, "trow")),
        check_vma=False,
    )
```

```python
import functools

import jax
import jax.numpy as jnp
from jax import lax
from jax.experimental import pallas as pl
from jax.experimental.pallas import tpu as pltpu
from jax.sharding import PartitionSpec as P

RBLK = 256
NT = 1024
MESH = pl.DeviceIdType.MESH
F32 = jnp.float32
BF16 = jnp.bfloat16


def contract_last(left_side, right_side):
    return lax.dot_general(
        left_side, right_side, (((1,), (1,)), ((), ())), preferred_element_type=F32
    )


def contract_inner(left_side, right_side):
    return lax.dot_general(
        left_side, right_side, (((1,), (0,)), ((), ())), preferred_element_type=F32
    )


def sin_cos(angle):
    turns = jnp.floor(angle * 0.6366197723675814 + 0.5)
    rest = angle - turns * 1.5703125
    rest = rest - turns * 4.837512969970703e-4
    rest = rest - turns * 7.549789948768648e-8
    square = rest * rest
    sine = rest + rest * square * (
        -1.6666654611e-1 + square * (8.3321608736e-3 - square * 1.9515295891e-4)
    )
    cosine = 1.0 - 0.5 * square + square * square * (
        4.166664568298827e-2 + square * (-1.388731625493765e-3 + square * 2.443315711809948e-5)
    )
    quarter = turns - 4.0 * jnp.floor(turns * 0.25)
    swap = (quarter == 1.0) | (quarter == 3.0)
    first = jnp.where(swap, cosine, sine)
    second = jnp.where(swap, sine, cosine)
    first = jnp.where(quarter >= 2.0, -first, first)
    second = jnp.where((quarter == 1.0) | (quarter == 2.0), -second, second)
    return first, second


def prefix_sums(phi, count):
    sine, cosine = sin_cos(phi)
    sine_n, cosine_n = sin_cos(count * phi)
    still = phi == 0.0
    ratio = jnp.where(still, count, sine_n / jnp.where(still, 1.0, sine))
    cos_sum = ratio * (cosine_n * cosine + sine_n * sine)
    sin_sum = ratio * (sine_n * cosine - cosine_n * sine)
    return cos_sum, sin_sum


def gram(onset, omega_a, omega_b):
    count = onset.astype(F32)
    omega_a = jnp.full(count.shape, omega_a, F32)
    omega_b = jnp.full(count.shape, omega_b, F32)
    cos_aa, sin_aa = prefix_sums(omega_a, count)
    cos_bb, sin_bb = prefix_sums(omega_b, count)
    cos_sum, sin_sum = prefix_sums(0.5 * (omega_a + omega_b), count)
    cos_dif, sin_dif = prefix_sums(0.5 * (omega_a - omega_b), count)
    scale = 1.0 / NT
    g = {}
    g[0, 0] = scale * (count + cos_aa)
    g[1, 1] = scale * (count - cos_aa)
    g[0, 1] = -scale * sin_aa
    g[2, 2] = scale * (count + cos_bb)
    g[3, 3] = scale * (count - cos_bb)
    g[2, 3] = -scale * sin_bb
    g[0, 2] = scale * (cos_dif + cos_sum)
    g[1, 3] = scale * (cos_dif - cos_sum)
    g[0, 3] = -scale * (sin_sum - sin_dif)
    g[1, 2] = -scale * (sin_sum + sin_dif)
    for m in range(4):
        for n in range(m):
            g[m, n] = g[n, m]
    return g


def apply_gram(g, y):
    return [
        g[m, 0] * y[0] + g[m, 1] * y[1] + g[m, 2] * y[2] + g[m, 3] * y[3] for m in range(4)
    ]


def from_zero(me, count):
    return [step + (step + count - me) // count for step in range(count - 1)]


def kernel(
    n_row, n_col,
    start_hbm, u_hbm, v_hbm, rank_ref, onset_r_hbm, onset_s_hbm, omega_hbm,
    plus_ref, minus_ref,
    start_buf, u_buf, v_buf, omega_ref, onset_buf, gram_buf,
    recv1, hand1, back1, recv2, hand2, back2,
    local_sem, ssem, rsem,
):
    row = lax.axis_index("trow")
    col = lax.axis_index("tcol")
    freq = lax.axis_index("tm")
    me_r, me_s = col * 2 + freq, row * 2 + freq
    half = u_buf.shape[1] // 2

    for place, source, target in (
        (0, start_hbm.at[0], start_buf),
        (0, v_hbm.at[0, 0], v_buf.at[0]),
        (4, v_hbm.at[0, 1], v_buf.at[1]),
        (1, omega_hbm, omega_ref),
        (2, u_hbm.at[0, :, pl.ds(0, half)], u_buf.at[:, pl.ds(0, half)]),
        (3, u_hbm.at[0, :, pl.ds(half, half)], u_buf.at[:, pl.ds(half, half)]),
        (1, onset_r_hbm, onset_buf.at[0]),
        (1, onset_s_hbm, onset_buf.at[1]),
    ):
        pltpu.make_async_copy(source, target, local_sem.at[place]).start()

    def await_all(ref, sem):
        pltpu.make_async_copy(ref, ref, sem).wait()

    hubs_r = [{"tcol": place, "tm": 1} for place in from_zero(col, n_col)]
    hubs_s = [{"trow": place, "tm": 1} for place in from_zero(row, n_row)]
    barrier = pltpu.get_barrier_semaphore()

    def signal(device):
        pl.semaphore_signal(barrier, inc=1, device_id=device, device_id_type=MESH)

    @pl.when(freq == 1)
    def _():
        for device in hubs_r + hubs_s:
            signal(device)
            signal({**device, "tm": 0})

    @pl.when(freq == 0)
    def _():
        for device in hubs_s:
            signal({**device, "tm": 0})

    signal({"tm": 1 - freq})

    def push(source, target, sem, device):
        pltpu.make_async_remote_copy(
            src_ref=source, dst_ref=target, send_sem=ssem, recv_sem=rsem.at[sem],
            device_id=device, device_id_type=MESH,
        ).start()

    spans = [pl.ds(part * half, half) for part in range(2)]

    def push_half(part, device):
        piece = recv1.at[me_r, :, spans[part]]
        push(piece, piece, 4 + freq if part else 3 * freq, device)

    def add(recv, places):
        total = recv[places[0]].astype(F32)
        for place in places[1:]:
            total = total + recv[place].astype(F32)
        return [total[:8], total[8:]]

    entries = [(m, n) for m in range(4) for n in range(m, 4)]

    def kept_gram(side):
        g = {}
        for place, (m, n) in enumerate(entries):
            g[m, n] = g[n, m] = gram_buf[side, place]
        return g

    await_all(start_buf, local_sem.at[0])
    await_all(v_buf.at[0], local_sem.at[0])
    rows_in = jnp.concatenate([start_buf[0], start_buf[1]], axis=0).astype(BF16)
    first_real = contract_last(rows_in, v_buf[0])
    await_all(v_buf.at[1], local_sem.at[4])
    first_imag = contract_last(rows_in, v_buf[1])
    lane = lax.broadcasted_iota(jnp.int32, (8, first_real.shape[1]), 1)
    keep = lane < rank_ref[0, 0, 0] * RBLK
    t_real = jnp.where(keep, first_real[:8] - first_imag[8:], 0.0)
    t_imag = jnp.where(keep, first_imag[:8] + first_real[8:], 0.0)
    packed = jnp.concatenate([t_real, t_imag], axis=0).astype(BF16)

    for part in range(2):
        span = pl.ds(part * half, half)
        await_all(u_buf.at[:, span], local_sem.at[2 + part])
        second_real = contract_last(packed, u_buf[0, span])
        second_imag = contract_last(packed, u_buf[1, span])
        recv1[me_r, :, span] = jnp.concatenate(
            [second_real[:8] - second_imag[8:], second_imag[:8] + second_real[8:]], axis=0
        ).astype(BF16)
        if part == 0:
            pl.semaphore_wait(barrier, n_row + n_col - 1 + (1 - freq) * (n_row - 1))
        push_half(part, hubs_r[0])
    await_all(onset_buf, local_sem.at[1])
    pltpu.make_async_copy(omega_hbm, omega_ref, local_sem.at[1]).wait()

    @pl.when(freq == 0)
    def _():
        for part in range(2):
            push_half(part, {"tm": 1})

    for side in (0,):
        g = gram(onset_buf[side], omega_ref[0], omega_ref[1])
        for place, entry in enumerate(entries):
            gram_buf[side, place] = g[entry]

    for device in hubs_r[1:]:
        for part in range(2):
            push_half(part, device)

    for side in (1,):
        g = gram(onset_buf[side], omega_ref[0], omega_ref[1])
        for place, entry in enumerate(entries):
            gram_buf[side, place] = g[entry]

    @pl.when(freq == 1)
    def _():
        for part, span in enumerate(spans):
            g = {
                entry: gram_buf[0, place, :, span] for place, entry in enumerate(entries)
            }
            g.update({(n, m): value for (m, n), value in g.items()})
            await_all(recv1.at[pl.ds(0, n_col - 1), :, span], rsem.at[3 + 2 * part])
            near = add(recv1.at[:, :, span], range(1, 2 * n_col, 2))
            near = [g[m, 2] * near[0] + g[m, 3] * near[1] for m in range(4)]
            await_all(recv1.at[pl.ds(0, n_col), :, span], rsem.at[4 * part])
            y = add(recv1.at[:, :, span], range(0, 2 * n_col, 2))
            done = [g[m, 0] * y[0] + g[m, 1] * y[1] + near[m] for m in range(4)]
            hand1[:, span] = jnp.concatenate(done[:2], axis=0).astype(BF16)
            push(hand1.at[:, span], back1.at[:, span], 4 * part, {"tm": 0})
            back1[:, span] = jnp.concatenate(done[2:], axis=0).astype(BF16)

    first_real, first_imag = 0.0, 0.0
    for part, span in enumerate(spans):

        @pl.when(freq == 0)
        def _():
            await_all(back1.at[:, span], rsem.at[4 * part])

        rows_part = back1[:, span]
        first_real = first_real + contract_inner(rows_part, u_buf[0, span])
        first_imag = first_imag + contract_inner(rows_part, u_buf[1, span])
    rows_back = back1[...]
    s_real = jnp.where(keep, first_real[:8] + first_imag[8:], 0.0)
    s_imag = jnp.where(keep, first_real[8:] - first_imag[:8], 0.0)
    packed_back = jnp.concatenate([s_real, s_imag], axis=0).astype(BF16)
    half_s = v_buf.shape[2] // 2
    for part in range(2):
        span = pl.ds(part * half_s, half_s)
        second_real = contract_inner(packed_back, v_buf[0, :, span])
        second_imag = contract_inner(packed_back, v_buf[1, :, span])
        recv2[me_s, :, span] = jnp.concatenate(
            [second_real[:8] + second_imag[8:], second_real[8:] - second_imag[:8]], axis=0
        ).astype(BF16)

        @pl.when(freq == 0)
        def _():
            push(recv2.at[me_s, :, span], recv2.at[me_s, :, span], 1, {**hubs_s[0], "tm": 0})
    own = [2 * place for place in range(n_row)]
    far = [2 * place + 1 for place in range(n_row)]

    @pl.when(freq == 0)
    def _():
        push(recv2.at[me_s], recv2.at[me_s], 1, hubs_s[0])
        for tm in (0, 1):
            for device in hubs_s[1:]:
                push(recv2.at[me_s], recv2.at[me_s], 1, {**device, "tm": tm})
        push(recv2.at[me_s], recv2.at[me_s], 1, {"tm": 1})
        minus_ref[0, 0] = rows_back[:8]
        minus_ref[0, 1] = rows_back[8:]
        await_all(hand2, rsem.at[2])
        await_all(recv2.at[pl.ds(0, n_row - 1)], rsem.at[1])
        g, y = kept_gram(1), add(recv2, own)
        last = hand2[...].astype(F32)
        last = [last[:8], last[8:]]
        for m in range(2):
            plus_ref[0, m] = start_buf[m] - (g[m, 0] * y[0] + g[m, 1] * y[1] + last[m])

    @pl.when(freq == 1)
    def _():
        for device in hubs_s:
            push(recv2.at[me_s], recv2.at[me_s], 2, device)
        minus_ref[0, 0] = rows_back[:8]
        minus_ref[0, 1] = rows_back[8:]
        await_all(recv2.at[pl.ds(0, n_row - 1)], rsem.at[2])
        g, y = kept_gram(1), add(recv2, far)
        back2[...] = jnp.concatenate(
            [g[m, 2] * y[0] + g[m, 3] * y[1] for m in range(2)], axis=0
        ).astype(BF16)
        push(back2, hand2, 2, {"tm": 0})
        await_all(recv2.at[pl.ds(0, n_row)], rsem.at[1])
        x = add(recv2, own)
        done = apply_gram(g, x + y)
        for m in range(2):
            plus_ref[0, m] = start_buf[m] - done[2 + m]

    await_all(recv1.at[pl.ds(0, n_col)], ssem)
    await_all(recv2.at[pl.ds(0, n_row)], ssem)

    @pl.when(freq == 0)
    def _():
        await_all(recv2.at[pl.ds(0, n_row - 1)], ssem)


def epilogue(plus_ref, minus_ref, plus_out, minus_out, sem):
    copies = [
        pltpu.make_async_copy(plus_ref, plus_out, sem.at[0]),
        pltpu.make_async_copy(minus_ref, minus_out, sem.at[1]),
    ]
    for copy in copies:
        copy.start()
    for copy in copies:
        copy.wait()


def per_device(start_field, u_tiles, v_tiles, rank_blocks, onset_receiver, onset_source, omega):
    n_row = lax.axis_size("trow")
    n_col = lax.axis_size("tcol")
    tile_r, tile_s = u_tiles.shape[2], v_tiles.shape[3]
    hbm = pl.BlockSpec(memory_space=pl.ANY)
    vmem = pl.BlockSpec(memory_space=pltpu.VMEM)
    sems = pltpu.SemaphoreType.DMA
    shapes = (
        jax.ShapeDtypeStruct((1, 2, 8, tile_s), F32),
        jax.ShapeDtypeStruct((1, 2, 8, tile_r), BF16),
    )
    plus, minus = pl.pallas_call(
        functools.partial(kernel, n_row, n_col),
        out_shape=shapes,
        in_specs=[hbm] * 3 + [pl.BlockSpec(memory_space=pltpu.SMEM)] + [hbm] * 3,
        out_specs=(vmem, vmem),
        scratch_shapes=[
            pltpu.VMEM(start_field.shape[1:], F32),
            pltpu.VMEM(u_tiles.shape[1:], BF16),
            pltpu.VMEM(v_tiles.shape[1:], BF16),
            pltpu.SMEM((2,), F32),
            pltpu.VMEM((2, 8, tile_r), jnp.int32),
            pltpu.VMEM((2, 10, 8, tile_r), F32),
            pltpu.VMEM((2 * n_col, 16, tile_r), BF16),
            pltpu.VMEM((16, tile_r), BF16),
            pltpu.VMEM((16, tile_r), BF16),
            pltpu.VMEM((2 * n_row, 16, tile_s), BF16),
            pltpu.VMEM((16, tile_s), BF16),
            pltpu.VMEM((16, tile_s), BF16),
            sems((5,)),
            sems(()),
            sems((6,)),
        ],
        compiler_params=pltpu.CompilerParams(
            collective_id=0, has_side_effects=True, vmem_limit_bytes=24 * 1024 * 1024
        ),
    )(
        pin(start_field), pin(u_tiles), pin(v_tiles), rank_blocks,
        pin(onset_receiver), pin(onset_source), pin(omega),
    )
    return pl.pallas_call(
        epilogue,
        out_shape=shapes,
        in_specs=[vmem, vmem],
        out_specs=(pl.BlockSpec(memory_space=pltpu.HBM),) * 2,
        scratch_shapes=[sems((2,))],
    )(
        pltpu.with_memory_space_constraint(plus, pltpu.VMEM),
        pltpu.with_memory_space_constraint(minus, pltpu.VMEM),
    )


def pin(x):
    return pltpu.with_memory_space_constraint(x, pltpu.MemorySpace.HBM)


def solution(mesh):
    placed = (
        P("tm", None, None, "tcol"),
        P("tm", None, "trow", "tcol"),
        P("tm", None, "trow", "tcol"),
        P("tm", "trow", "tcol"),
        P(None, "trow"),
        P(None, "tcol"),
        P(),
    )
    return jax.shard_map(
        per_device,
        mesh=mesh,
        in_specs=placed,
        out_specs=(P("tm", None, None, "tcol"), P("tm", None, None, "trow")),
        check_vma=False,
    )
```

```python
import functools

import jax
import jax.numpy as jnp
from jax import lax
from jax.experimental import pallas as pl
from jax.experimental.pallas import tpu as pltpu
from jax.sharding import PartitionSpec as P

RBLK = 256
NT = 1024
MESH = pl.DeviceIdType.MESH
F32 = jnp.float32
BF16 = jnp.bfloat16


def contract_last(left_side, right_side):
    return lax.dot_general(
        left_side, right_side, (((1,), (1,)), ((), ())), preferred_element_type=F32
    )


def contract_inner(left_side, right_side):
    return lax.dot_general(
        left_side, right_side, (((1,), (0,)), ((), ())), preferred_element_type=F32
    )


def sin_cos(angle):
    turns = jnp.floor(angle * 0.6366197723675814 + 0.5)
    rest = angle - turns * 1.5703125
    rest = rest - turns * 4.837512969970703e-4
    rest = rest - turns * 7.549789948768648e-8
    square = rest * rest
    sine = rest + rest * square * (
        -1.6666654611e-1 + square * (8.3321608736e-3 - square * 1.9515295891e-4)
    )
    cosine = 1.0 - 0.5 * square + square * square * (
        4.166664568298827e-2 + square * (-1.388731625493765e-3 + square * 2.443315711809948e-5)
    )
    quarter = turns - 4.0 * jnp.floor(turns * 0.25)
    swap = (quarter == 1.0) | (quarter == 3.0)
    first = jnp.where(swap, cosine, sine)
    second = jnp.where(swap, sine, cosine)
    first = jnp.where(quarter >= 2.0, -first, first)
    second = jnp.where((quarter == 1.0) | (quarter == 2.0), -second, second)
    return first, second


def prefix_sums(phi, count):
    sine, cosine = sin_cos(phi)
    sine_n, cosine_n = sin_cos(count * phi)
    still = phi == 0.0
    ratio = jnp.where(still, count, sine_n / jnp.where(still, 1.0, sine))
    cos_sum = ratio * (cosine_n * cosine + sine_n * sine)
    sin_sum = ratio * (sine_n * cosine - cosine_n * sine)
    return cos_sum, sin_sum


def gram(onset, omega_a, omega_b):
    count = onset.astype(F32)
    omega_a = jnp.full(count.shape, omega_a, F32)
    omega_b = jnp.full(count.shape, omega_b, F32)
    cos_aa, sin_aa = prefix_sums(omega_a, count)
    cos_bb, sin_bb = prefix_sums(omega_b, count)
    cos_sum, sin_sum = prefix_sums(0.5 * (omega_a + omega_b), count)
    cos_dif, sin_dif = prefix_sums(0.5 * (omega_a - omega_b), count)
    scale = 1.0 / NT
    g = {}
    g[0, 0] = scale * (count + cos_aa)
    g[1, 1] = scale * (count - cos_aa)
    g[0, 1] = -scale * sin_aa
    g[2, 2] = scale * (count + cos_bb)
    g[3, 3] = scale * (count - cos_bb)
    g[2, 3] = -scale * sin_bb
    g[0, 2] = scale * (cos_dif + cos_sum)
    g[1, 3] = scale * (cos_dif - cos_sum)
    g[0, 3] = -scale * (sin_sum - sin_dif)
    g[1, 2] = -scale * (sin_sum + sin_dif)
    for m in range(4):
        for n in range(m):
            g[m, n] = g[n, m]
    return g


def apply_gram(g, y):
    return [
        g[m, 0] * y[0] + g[m, 1] * y[1] + g[m, 2] * y[2] + g[m, 3] * y[3] for m in range(4)
    ]


def from_zero(me, count):
    return [step + (step + count - me) // count for step in range(count - 1)]


def kernel(
    n_row, n_col,
    start_hbm, u_hbm, v_hbm, rank_ref, onset_r_hbm, onset_s_hbm, omega_hbm,
    plus_ref, minus_ref,
    start_buf, u_buf, v_buf, omega_ref, onset_buf, gram_buf,
    recv1, hand1, back1, recv2, hand2, back2,
    local_sem, ssem, rsem,
):
    row = lax.axis_index("trow")
    col = lax.axis_index("tcol")
    freq = lax.axis_index("tm")
    me_r, me_s = col * 2 + freq, row * 2 + freq
    half = u_buf.shape[1] // 2

    for place, source, target in (
        (0, start_hbm.at[0], start_buf),
        (0, v_hbm.at[0, 0], v_buf.at[0]),
        (4, v_hbm.at[0, 1], v_buf.at[1]),
        (1, omega_hbm, omega_ref),
        (2, u_hbm.at[0, :, pl.ds(0, half)], u_buf.at[:, pl.ds(0, half)]),
        (3, u_hbm.at[0, :, pl.ds(half, half)], u_buf.at[:, pl.ds(half, half)]),
        (1, onset_r_hbm, onset_buf.at[0]),
        (1, onset_s_hbm, onset_buf.at[1]),
    ):
        pltpu.make_async_copy(source, target, local_sem.at[place]).start()

    def await_all(ref, sem):
        pltpu.make_async_copy(ref, ref, sem).wait()

    hubs_r = [{"tcol": place, "tm": 1} for place in from_zero(col, n_col)]
    hubs_s = [{"trow": place, "tm": 1} for place in from_zero(row, n_row)]
    barrier = pltpu.get_barrier_semaphore()

    def signal(device):
        pl.semaphore_signal(barrier, inc=1, device_id=device, device_id_type=MESH)

    @pl.when(freq == 1)
    def _():
        for device in hubs_r + hubs_s:
            signal(device)
            signal({**device, "tm": 0})

    @pl.when(freq == 0)
    def _():
        for device in hubs_s:
            signal({**device, "tm": 0})

    signal({"tm": 1 - freq})

    def push(source, target, sem, device):
        pltpu.make_async_remote_copy(
            src_ref=source, dst_ref=target, send_sem=ssem, recv_sem=rsem.at[sem],
            device_id=device, device_id_type=MESH,
        ).start()

    def add(recv, places):
        total = recv[places[0]].astype(F32)
        for place in places[1:]:
            total = total + recv[place].astype(F32)
        return [total[:8], total[8:]]

    entries = [(m, n) for m in range(4) for n in range(m, 4)]

    def kept_gram(side):
        g = {}
        for place, (m, n) in enumerate(entries):
            g[m, n] = g[n, m] = gram_buf[side, place]
        return g

    await_all(start_buf, local_sem.at[0])
    await_all(v_buf.at[0], local_sem.at[0])
    rows_in = jnp.concatenate([start_buf[0], start_buf[1]], axis=0).astype(BF16)
    first_real = contract_last(rows_in, v_buf[0])
    await_all(v_buf.at[1], local_sem.at[4])
    first_imag = contract_last(rows_in, v_buf[1])
    lane = lax.broadcasted_iota(jnp.int32, (8, first_real.shape[1]), 1)
    keep = lane < rank_ref[0, 0, 0] * RBLK
    t_real = jnp.where(keep, first_real[:8] - first_imag[8:], 0.0)
    t_imag = jnp.where(keep, first_imag[:8] + first_real[8:], 0.0)
    packed = jnp.concatenate([t_real, t_imag], axis=0).astype(BF16)

    for part in range(2):
        span = pl.ds(part * half, half)
        await_all(u_buf.at[:, span], local_sem.at[2 + part])
        second_real = contract_last(packed, u_buf[0, span])
        second_imag = contract_last(packed, u_buf[1, span])
        recv1[me_r, :, span] = jnp.concatenate(
            [second_real[:8] - second_imag[8:], second_imag[:8] + second_real[8:]], axis=0
        ).astype(BF16)
        if part == 0:
            pl.semaphore_wait(barrier, n_row + n_col - 1 + (1 - freq) * (n_row - 1))
        push(recv1.at[me_r, :, span], recv1.at[me_r, :, span], 3 * freq, hubs_r[0])
    await_all(onset_buf, local_sem.at[1])
    pltpu.make_async_copy(omega_hbm, omega_ref, local_sem.at[1]).wait()

    @pl.when(freq == 0)
    def _():
        push(recv1.at[me_r], recv1.at[me_r], 0, {"tm": 1})
        for device in hubs_r[1:]:
            push(recv1.at[me_r], recv1.at[me_r], 0, device)

    for side in (0,):
        g = gram(onset_buf[side], omega_ref[0], omega_ref[1])
        for place, entry in enumerate(entries):
            gram_buf[side, place] = g[entry]

    @pl.when(freq == 1)
    def _():
        for device in hubs_r[1:]:
            push(recv1.at[me_r], recv1.at[me_r], 3, device)

    for side in (1,):
        g = gram(onset_buf[side], omega_ref[0], omega_ref[1])
        for place, entry in enumerate(entries):
            gram_buf[side, place] = g[entry]

    @pl.when(freq == 0)
    def _():
        await_all(back1, rsem.at[0])

    @pl.when(freq == 1)
    def _():
        g = kept_gram(0)
        await_all(recv1.at[pl.ds(0, n_col - 1)], rsem.at[3])
        near = add(recv1, range(1, 2 * n_col, 2))
        near = [g[m, 2] * near[0] + g[m, 3] * near[1] for m in range(4)]
        await_all(recv1.at[pl.ds(0, n_col)], rsem.at[0])
        y = add(recv1, range(0, 2 * n_col, 2))
        hand1[...] = jnp.concatenate(
            [g[m, 0] * y[0] + g[m, 1] * y[1] + near[m] for m in range(2)], axis=0
        ).astype(BF16)
        push(hand1, back1, 0, {"tm": 0})
        back1[...] = jnp.concatenate(
            [g[m, 0] * y[0] + g[m, 1] * y[1] + near[m] for m in (2, 3)], axis=0
        ).astype(BF16)

    rows_back = back1[...]
    first_real = contract_inner(rows_back, u_buf[0])
    first_imag = contract_inner(rows_back, u_buf[1])
    s_real = jnp.where(keep, first_real[:8] + first_imag[8:], 0.0)
    s_imag = jnp.where(keep, first_real[8:] - first_imag[:8], 0.0)
    packed_back = jnp.concatenate([s_real, s_imag], axis=0).astype(BF16)
    half_s = v_buf.shape[2] // 2
    for part in range(2):
        span = pl.ds(part * half_s, half_s)
        second_real = contract_inner(packed_back, v_buf[0, :, span])
        second_imag = contract_inner(packed_back, v_buf[1, :, span])
        recv2[me_s, :, span] = jnp.concatenate(
            [second_real[:8] + second_imag[8:], second_real[8:] - second_imag[:8]], axis=0
        ).astype(BF16)

        @pl.when(freq == 0)
        def _():
            push(recv2.at[me_s, :, span], recv2.at[me_s, :, span], 1, {**hubs_s[0], "tm": 0})
    own = [2 * place for place in range(n_row)]
    far = [2 * place + 1 for place in range(n_row)]

    @pl.when(freq == 0)
    def _():
        push(recv2.at[me_s], recv2.at[me_s], 1, hubs_s[0])
        for tm in (0, 1):
            for device in hubs_s[1:]:
                push(recv2.at[me_s], recv2.at[me_s], 1, {**device, "tm": tm})
        push(recv2.at[me_s], recv2.at[me_s], 1, {"tm": 1})
        minus_ref[0, 0] = rows_back[:8]
        minus_ref[0, 1] = rows_back[8:]
        await_all(hand2, rsem.at[2])
        await_all(recv2.at[pl.ds(0, n_row - 1)], rsem.at[1])
        g, y = kept_gram(1), add(recv2, own)
        last = hand2[...].astype(F32)
        last = [last[:8], last[8:]]
        for m in range(2):
            plus_ref[0, m] = start_buf[m] - (g[m, 0] * y[0] + g[m, 1] * y[1] + last[m])

    @pl.when(freq == 1)
    def _():
        for device in hubs_s:
            push(recv2.at[me_s], recv2.at[me_s], 2, device)
        minus_ref[0, 0] = rows_back[:8]
        minus_ref[0, 1] = rows_back[8:]
        await_all(recv2.at[pl.ds(0, n_row - 1)], rsem.at[2])
        g, y = kept_gram(1), add(recv2, far)
        back2[...] = jnp.concatenate(
            [g[m, 2] * y[0] + g[m, 3] * y[1] for m in range(2)], axis=0
        ).astype(BF16)
        push(back2, hand2, 2, {"tm": 0})
        await_all(recv2.at[pl.ds(0, n_row)], rsem.at[1])
        x = add(recv2, own)
        done = apply_gram(g, x + y)
        for m in range(2):
            plus_ref[0, m] = start_buf[m] - done[2 + m]

    await_all(recv1.at[pl.ds(0, n_col)], ssem)
    await_all(recv2.at[pl.ds(0, n_row)], ssem)

    @pl.when(freq == 0)
    def _():
        await_all(recv2.at[pl.ds(0, n_row - 1)], ssem)


def epilogue(plus_ref, minus_ref, plus_out, minus_out, sem):
    copies = [
        pltpu.make_async_copy(plus_ref, plus_out, sem.at[0]),
        pltpu.make_async_copy(minus_ref, minus_out, sem.at[1]),
    ]
    for copy in copies:
        copy.start()
    for copy in copies:
        copy.wait()


def per_device(start_field, u_tiles, v_tiles, rank_blocks, onset_receiver, onset_source, omega):
    n_row = lax.axis_size("trow")
    n_col = lax.axis_size("tcol")
    tile_r, tile_s = u_tiles.shape[2], v_tiles.shape[3]
    hbm = pl.BlockSpec(memory_space=pl.ANY)
    vmem = pl.BlockSpec(memory_space=pltpu.VMEM)
    sems = pltpu.SemaphoreType.DMA
    shapes = (
        jax.ShapeDtypeStruct((1, 2, 8, tile_s), F32),
        jax.ShapeDtypeStruct((1, 2, 8, tile_r), BF16),
    )
    plus, minus = pl.pallas_call(
        functools.partial(kernel, n_row, n_col),
        out_shape=shapes,
        in_specs=[hbm] * 3 + [pl.BlockSpec(memory_space=pltpu.SMEM)] + [hbm] * 3,
        out_specs=(vmem, vmem),
        scratch_shapes=[
            pltpu.VMEM(start_field.shape[1:], F32),
            pltpu.VMEM(u_tiles.shape[1:], BF16),
            pltpu.VMEM(v_tiles.shape[1:], BF16),
            pltpu.SMEM((2,), F32),
            pltpu.VMEM((2, 8, tile_r), jnp.int32),
            pltpu.VMEM((2, 10, 8, tile_r), F32),
            pltpu.VMEM((2 * n_col, 16, tile_r), BF16),
            pltpu.VMEM((16, tile_r), BF16),
            pltpu.VMEM((16, tile_r), BF16),
            pltpu.VMEM((2 * n_row, 16, tile_s), BF16),
            pltpu.VMEM((16, tile_s), BF16),
            pltpu.VMEM((16, tile_s), BF16),
            sems((5,)),
            sems(()),
            sems((4,)),
        ],
        compiler_params=pltpu.CompilerParams(
            collective_id=0, has_side_effects=True, vmem_limit_bytes=24 * 1024 * 1024
        ),
    )(
        pin(start_field), pin(u_tiles), pin(v_tiles), rank_blocks,
        pin(onset_receiver), pin(onset_source), pin(omega),
    )
    return pl.pallas_call(
        epilogue,
        out_shape=shapes,
        in_specs=[vmem, vmem],
        out_specs=(pl.BlockSpec(memory_space=pltpu.HBM),) * 2,
        scratch_shapes=[sems((2,))],
    )(
        pltpu.with_memory_space_constraint(plus, pltpu.VMEM),
        pltpu.with_memory_space_constraint(minus, pltpu.VMEM),
    )


def pin(x):
    return pltpu.with_memory_space_constraint(x, pltpu.MemorySpace.HBM)


def solution(mesh):
    placed = (
        P("tm", None, None, "tcol"),
        P("tm", None, "trow", "tcol"),
        P("tm", None, "trow", "tcol"),
        P("tm", "trow", "tcol"),
        P(None, "trow"),
        P(None, "tcol"),
        P(),
    )
    return jax.shard_map(
        per_device,
        mesh=mesh,
        in_specs=placed,
        out_specs=(P("tm", None, None, "tcol"), P("tm", None, None, "trow")),
        check_vma=False,
    )
```
